512 devices in a mesh: dp: 4 (over z_lo, core), seq: 8 (over y), vocab: 16 (over z_hi, x).
Axes of the slice: x: 4, y: 8, z: 8 (z_hi: 4, z_lo: 2; z = z_hi * 2 + z_lo), core: 2. Of those that a mesh axis runs over, the one named last changes fastest.
Arguments:
- queries: bfloat16 [4, 256, 4096], P('dp', 'seq', 'vocab'), may hold values from -64 to 64
- enc_keys: bfloat16 [4, 1024, 4096], P('dp', 'seq', 'vocab'), may hold values from -6 to 6
- enc_values: bfloat16 [4, 1024, 4096], P('dp', 'seq', 'vocab'), may hold values from -6 to 6
- enc_lengths: int32 [4], P('dp'), may hold values from 256 to 1024, as said below
- out_proj: bfloat16 [4096, 4096], P('vocab', 'seq'), may hold values from -0.375 to 0.375
- residual: bfloat16 [4, 256, 4096], P('dp', None, 'seq'), may hold values from -270 to 270
- norm_gain: float32 [4096], P('seq'), may hold values from 0.4 to 1.6
- head_weight: bfloat16 [4096, 32128], P('seq', 'vocab'), may hold values from -1 to 1
- targets: int32 [4, 256], P('dp', 'seq'), may hold values from 0 to 32127
Outputs:
- mean_loss: float32 [], replicated
- head_grad: bfloat16 [4096, 32128], P('seq', 'vocab')
- key_grad: float32 [4, 1024, 4096], P('dp', 'seq', 'vocab')
- value_grad: float32 [4, 1024, 4096], P('dp', 'seq', 'vocab')
The draws below stay inside these ranges and needn't reach their ends.
Inputs may be any that keep to these rules, and one draw needn't show every extreme that they name: `enc_lengths`: each example has at least 256 unpadded positions; some example has none padded.
All inputs are finite; a program needn't handle non-finite values.
Results may differ from the reference program's by a relative error of at most 0.02.
Values may be sent and summed in bfloat16 or wider, within the bound.
A program may use at most 64 MiB of HBM per device.

```python
import math
import jax
import jax.numpy as jnp
import numpy as np
from jax import lax

D = 4096
HEADS = 16
HDIM = 256
VOCAB = 32128
EX = 1
TGT_DEV = 32
BATCH = 4
TGT = 256
ENC = 1024
N_DP = 4
N_SEQ = 8


def sign_pattern(key):
    chosen = jax.random.bernoulli(jax.random.fold_in(key, 501), 0.5, (D,))
    return jnp.where(chosen, 1.0, -1.0).astype(jnp.float32)


def width_profile():
    position = lax.broadcasted_iota(jnp.float32, (D,), 0) / D
    profile = 0.4 + 1.6 * position
    return profile


def encoder_draw(key):
    base_key = jax.random.fold_in(key, 101)
    full_shape = (BATCH, ENC, HEADS * HDIM)
    drawn = jnp.clip(jax.random.normal(base_key, full_shape, jnp.float32), -6.0, 6.0)
    return drawn


def leading_keys(key):
    drawn = encoder_draw(key)
    return drawn


def draw_enc_keys(key, part):
    drawn = leading_keys(key)
    return drawn.astype(jnp.bfloat16)


def draw_queries(key, part):
    base_key = jax.random.fold_in(key, 201)
    full_shape = (BATCH, TGT, HEADS * HDIM)
    drawn = jnp.clip(2.0 * jax.random.normal(base_key, full_shape, jnp.float32), -12.0, 12.0)
    return drawn.astype(jnp.bfloat16)


def draw_enc_lengths(key, part):
    lengths = jax.random.randint(jax.random.fold_in(key, 301), (BATCH,), ENC // 4, ENC + 1)
    longest = jax.random.randint(jax.random.fold_in(key, 302), (), 0, BATCH)
    shortest = (longest + 1 + jax.random.randint(jax.random.fold_in(key, 303), (), 0, BATCH - 1)) % BATCH
    example_ids = lax.broadcasted_iota(jnp.int32, (BATCH,), 0)
    lengths = jnp.where(example_ids == longest, ENC, lengths)
    lengths = jnp.where(example_ids == shortest, ENC // 4, lengths)
    return lengths.astype(jnp.int32)


def draw_residual(key, part):
    base_key = jax.random.fold_in(key, 401)
    full_shape = (BATCH, TGT, D)
    rising = 0.5 + lax.broadcasted_iota(jnp.float32, (D,), 0) / D
    pattern = sign_pattern(key)
    shared = pattern * width_profile()
    row_factor = jax.random.uniform(jax.random.fold_in(key, 405), (BATCH, TGT, 1), jnp.float32, -2.0, 2.0)
    noise = jnp.clip(jax.random.normal(base_key, full_shape, jnp.float32), -6.0, 6.0) * rising
    drawn = 0.7 * noise + row_factor * shared
    return drawn.astype(jnp.bfloat16)


def draw_head_weight(key, part):
    base_key = jax.random.fold_in(key, 601)
    full_shape = (D, VOCAB)
    rising = 0.5 + lax.broadcasted_iota(jnp.float32, (VOCAB,), 0) / VOCAB
    spread = 2.5 * D ** (-0.5)
    pattern = sign_pattern(key)
    column_factor = jnp.clip(jax.random.normal(jax.random.fold_in(key, 604), (VOCAB,), jnp.float32), -3.0, 3.0)
    shared = 12.0 / D * (pattern * width_profile())[:, None] * column_factor[None, :]
    drawn = jnp.clip(jax.random.normal(base_key, full_shape, jnp.float32), -6.0, 6.0) * spread * rising + shared
    return drawn.astype(jnp.bfloat16)


def set_ends(result, stream_key, least, top_value):
    dims = result.shape
    place = [jax.random.randint(jax.random.fold_in(stream_key, axis), (), 0, dims[axis]) for axis in range(len(dims))]
    result = result.at[tuple(place)].set(least)
    longest = dims.index(max(dims))
    place[longest] = (place[longest] + 1) % dims[longest]
    return result.at[tuple(place)].set(top_value)


def block_scale(stream_key, extent, split, smallest, high):
    factor_of = 1.0
    for dim, blocks in split:
        heights = jax.random.uniform(jax.random.fold_in(jax.random.fold_in(stream_key, 6), dim), (blocks,), jnp.float32, smallest / len(split), high / len(split))
        factor_of = factor_of * jnp.repeat(jnp.exp(heights), extent[dim] // blocks).reshape((-1,) + (1,) * (len(extent) - 1 - dim))
    return factor_of


def cumulative_ranks(amount, slope):
    weights = [(1 << 20) // math.isqrt(standing ** slope) + 1 for standing in range(1, amount + 1)]
    scale = 1 + sum(weights) // (1 << 30)
    return np.cumsum(np.array([max(1, weight // scale) for weight in weights]))


def ranked_ids(key, shape, amount, skew):
    listing = cumulative_ranks(amount, skew)
    pick = jax.random.randint(jax.random.fold_in(key, 1), shape, 0, int(listing[amount - 1]))
    grade = jnp.searchsorted(jnp.asarray(listing, jnp.int32), pick, side="right")
    return jax.random.permutation(jax.random.fold_in(key, 2), amount)[grade].astype(jnp.int32)


def scatter_about(key, shape, deviation, limit, cuts=(), kind=jnp.bfloat16):
    result = jax.random.normal(key, shape, jnp.float32) * deviation
    if len(cuts) > 0:
        result = block_scale(key, shape, cuts, -0.22, 0.18) * result
    return jnp.clip(result, min=-limit, max=limit).astype(kind)


def setup_inputs(seed: int = 0) -> dict:
    key_of = jax.random.split(jax.random.key(seed), 10)
    return {
        "queries": draw_queries(jax.random.fold_in(key_of[9], 71), 0),
        "enc_keys": draw_enc_keys(jax.random.fold_in(key_of[9], 71), 0),
        "enc_values": scatter_about(key_of[2], (BATCH, ENC, HEADS * HDIM), 1.0, 6.0, ((0, 4), (1, 8), (2, 16))),
        "enc_lengths": draw_enc_lengths(jax.random.fold_in(key_of[9], 71), 0),
        "out_proj": scatter_about(key_of[4], (HEADS * HDIM, D), (HEADS * HDIM // 16) ** -0.5, 0.375, ((0, 16), (1, 8))),
        "residual": draw_residual(jax.random.fold_in(key_of[9], 71), 0),
        "norm_gain": jnp.clip(1.0 + 0.12 * jax.random.normal(key_of[6], (D,), jnp.float32), 0.4, 1.6),
        "head_weight": draw_head_weight(jax.random.fold_in(key_of[9], 71), 0),
        "targets": set_ends(ranked_ids(key_of[8], (BATCH, TGT), VOCAB, 2), jax.random.fold_in(key_of[8], 3), 0, VOCAB - 1).astype(jnp.int32),
    }


zloss_weight = 0.0001
norm_epsilon = 1e-06

def settle(term):
    return lax.optimization_barrier(term.astype(jnp.bfloat16)).astype(jnp.float32)

def reference(queries, enc_keys, enc_values, enc_lengths, out_proj, residual, norm_gain, head_weight, targets):
    score_scale = HDIM ** (-0.5)

    def example_pass(inputs):
        query_rows, key_rows, value_rows, length, residual_rows, target_rows = inputs
        query_heads = query_rows.astype(jnp.float32).reshape(TGT, HEADS, HDIM)
        key_heads = key_rows.astype(jnp.float32).reshape(ENC, HEADS, HDIM)
        value_heads = value_rows.astype(jnp.float32).reshape(ENC, HEADS, HDIM)
        scores = jnp.einsum('thd,jhd->htj', query_heads, key_heads) * score_scale
        valid_keys = jnp.arange(ENC, dtype=jnp.int32) < length
        scores = jnp.where(valid_keys[None, None, :], scores, -jnp.inf)
        score_peak = lax.optimization_barrier(jnp.max(scores, axis=-1, keepdims=True))
        score_exp = jnp.exp(scores - score_peak)
        weights_full = score_exp / lax.optimization_barrier(jnp.sum(score_exp, axis=-1, keepdims=True))
        weights_half = weights_full.astype(jnp.bfloat16)
        attended = jnp.einsum('htj,jhd->thd', weights_half.astype(jnp.float32), value_heads)
        attended = attended.reshape(TGT, HEADS * HDIM).astype(jnp.bfloat16)
        mixed_rows = residual_rows.astype(jnp.float32) + jnp.dot(attended, out_proj, preferred_element_type=jnp.float32)
        square_sum = lax.optimization_barrier(jnp.sum(mixed_rows * mixed_rows, axis=-1))
        inverse_rms = lax.rsqrt(square_sum / D + norm_epsilon)
        normed = (mixed_rows * inverse_rms[:, None] * norm_gain).astype(jnp.bfloat16)
        logits = jnp.dot(normed, head_weight, preferred_element_type=jnp.float32)
        row_peak = lax.optimization_barrier(jnp.max(logits, axis=-1))
        log_total = row_peak + jnp.log(lax.optimization_barrier(jnp.sum(jnp.exp(logits - row_peak[:, None]), axis=-1)))
        target_hit = jnp.arange(VOCAB, dtype=jnp.int32)[None, :] == target_rows[:, None]
        target_logit = lax.optimization_barrier(jnp.sum(jnp.where(target_hit, logits, 0.0), axis=-1))
        token_loss = log_total - target_logit + zloss_weight * log_total * log_total
        logit_grad = (jnp.exp(logits - log_total[:, None]) * (1.0 + 2.0 * zloss_weight * log_total)[:, None] - target_hit.astype(jnp.float32)).astype(jnp.bfloat16)
        normed_grad = jnp.dot(logit_grad, head_weight.T, preferred_element_type=jnp.float32)
        gated = normed_grad * norm_gain
        dot_row = lax.optimization_barrier(jnp.sum(gated * mixed_rows, axis=-1))
        mixed_grad = (gated * inverse_rms[:, None] - mixed_rows * (inverse_rms ** 3 * dot_row / D)[:, None]).astype(jnp.bfloat16)
        attended_grad = jnp.dot(mixed_grad, out_proj.T, preferred_element_type=jnp.float32).astype(jnp.bfloat16)
        grad_heads = attended_grad.astype(jnp.float32).reshape(TGT, HEADS, HDIM)
        prob_grad = jnp.einsum('thd,jhd->htj', grad_heads, value_heads)
        score_grad = weights_full * (prob_grad - lax.optimization_barrier(jnp.sum(weights_full * prob_grad, axis=-1, keepdims=True)))
        score_half = (score_grad * score_scale).astype(jnp.bfloat16)
        block_weights = weights_half.astype(jnp.float32).reshape(HEADS, N_SEQ, TGT_DEV, ENC)
        block_scores = score_half.astype(jnp.float32).reshape(HEADS, N_SEQ, TGT_DEV, ENC)
        block_grads = grad_heads.reshape(N_SEQ, TGT_DEV, HEADS, HDIM)
        block_queries = query_heads.reshape(N_SEQ, TGT_DEV, HEADS, HDIM)
        value_part = jnp.einsum('hstj,sthd->sjhd', block_weights, block_grads)
        key_part = jnp.einsum('hstj,sthd->sjhd', block_scores, block_queries)
        value_grad = lax.optimization_barrier(jnp.sum(settle(value_part), axis=0)).reshape(ENC, HEADS * HDIM)
        key_grad = lax.optimization_barrier(jnp.sum(settle(key_part), axis=0)).reshape(ENC, HEADS * HDIM)
        return (token_loss, normed, logit_grad, key_grad, value_grad)
    token_losses, normed_all, grads_all, key_grad, value_grad = lax.map(example_pass, (queries, enc_keys, enc_values, enc_lengths, residual, targets))
    mean_loss = jnp.sum(token_losses) / (BATCH * TGT)

    def group_add(group, accumulated):
        normed_rows = lax.dynamic_slice_in_dim(normed_all, group * EX, EX, 0).reshape(EX * TGT, D)
        grad_rows = lax.dynamic_slice_in_dim(grads_all, group * EX, EX, 0).reshape(EX * TGT, VOCAB)
        return accumulated + settle(jnp.dot(normed_rows.T, grad_rows, preferred_element_type=jnp.float32))
    head_total = lax.fori_loop(0, N_DP, group_add, jnp.zeros((D, VOCAB), jnp.float32))
    return (mean_loss, head_total.astype(jnp.bfloat16), key_grad, value_grad)
```

```python
import functools
import types

import jax
import jax.numpy as jnp
from jax import lax
from jax.experimental import pallas as pl
from jax.experimental.pallas import tpu as pltpu
from jax.sharding import PartitionSpec as P

HDIM = 256
ZW = 0.0001
EPS = 1e-06
MESH = pl.DeviceIdType.MESH
F32 = jnp.float32
BF16 = jnp.bfloat16


def dot(a, b, ca, cb):
    return lax.dot_general(a, b, (((ca,), (cb,)), ((), ())), preferred_element_type=F32)


def eye(n, m):
    return lax.broadcasted_iota(jnp.int32, (n, m), 0) == lax.broadcasted_iota(jnp.int32, (n, m), 1)


def to_row(col, n):
    return jnp.sum(jnp.where(eye(n, 128), jnp.broadcast_to(col, (n, 128)), 0.0), axis=0, keepdims=True)


def to_col(row, n):
    return jnp.sum(jnp.where(eye(n, 128), jnp.broadcast_to(row, (n, 128)), 0.0), axis=1, keepdims=True)


def lane_pick(first, second, n):
    lane = lax.broadcasted_iota(jnp.int32, (n, 128), 1)
    return jnp.where(lane < 64, first, second)


def sub_pick(rows):
    sub = lax.broadcasted_iota(jnp.int32, (8, 128), 0)
    tile = jnp.zeros((8, 128), F32)
    for i, row in enumerate(rows):
        tile = jnp.where(sub == i, row, tile)
    return tile


def kernel(cfg, q, k, v, ln, wo, res, gain, w_hbm, tgt, out_loss, out_hg, out_kg, out_vg, *scratch):
    NS, NV, TR, KJ, C, V, VP, batch_rows = cfg
    b = types.SimpleNamespace(**dict(zip(scratch_list(cfg), scratch)))
    HD = HDIM
    R = TR * NS
    RB = R // NV
    NB = TR // RB
    H = NS // 2
    VH = VP // 2
    D = C * NS
    scale = HD ** (-0.5)
    md, ms, mv = lax.axis_index("dp"), lax.axis_index("seq"), lax.axis_index("vocab")
    core = lax.rem(md, 2)
    zlo = md // 2
    mate = md + 1 - 2 * core
    zmate = lax.rem(md + 2, 4)
    right, left = lax.rem(ms + 1, NS), lax.rem(ms + NS - 1, NS)
    ssem, rsem = b.ssem, b.rsem
    used = [0]

    def sem():
        used[0] += 1
        return ssem.at[used[0] - 1], rsem.at[used[0] - 1]

    def push(src, dst, axis, to, sems):
        copy = pltpu.make_async_remote_copy(
            src_ref=src, dst_ref=dst, send_sem=sems[0], recv_sem=sems[1],
            device_id={axis: to}, device_id_type=MESH)
        copy.start()
        return copy

    drains = []

    def wait_bytes(ref, one):
        pltpu.make_async_copy(ref, ref, one).wait()

    def spread(src, dst, axis):
        me, n = (ms, NS) if axis == "seq" else (mv, NV)
        sems = sem()
        for step in range(1, n):
            push(src, dst.at[me], axis, lax.rem(me + step, n), sems)
        rest = dst.at[pl.ds(0, n - 1)]
        drains.append((rest, sems[0]))
        return lambda: wait_bytes(rest, sems[1])

    def scatter(src, dst, axis):
        me, n = (ms, NS) if axis == "seq" else (mv, NV)
        sems = sem()
        for step in range(1, n):
            to = lax.rem(me + step, n)
            push(src.at[to], dst.at[step - 1], axis, to, sems)
        rest = dst.at[pl.ds(0, n - 1)]
        drains.append((rest, sems[0]))
        return lambda: wait_bytes(rest, sems[1])

    def one(src, dst, axis, to):
        copy = push(src, dst, axis, to, sem())
        drains.append(copy)
        return copy.wait_recv

    barrier = pltpu.get_barrier_semaphore()
    for step in range(1, NS):
        pl.semaphore_signal(barrier, inc=1, device_id={"seq": lax.rem(ms + step, NS)}, device_id_type=MESH)
    for step in range(1, NV):
        pl.semaphore_signal(barrier, inc=1, device_id={"vocab": lax.rem(mv + step, NV)}, device_id_type=MESH)
    for to in (mate, zmate):
        pl.semaphore_signal(barrier, inc=1, device_id={"dp": to}, device_id_type=MESH)
    w_copy = pltpu.make_async_copy(w_hbm, b.w_in, b.lsem.at[0])
    w_copy.start()
    pl.semaphore_wait(barrier, NS - 1 + NV - 1 + 2)

    got_q = spread(q, b.q_all, "seq")
    b.q_all[ms] = q[...]
    w_copy.wait()
    w = b.w
    tail = V // 128 * 128
    w[:, 0:tail] = b.w_in[:, 0:tail]
    if tail < VP:
        w[:, tail:VP] = jnp.zeros((C, VP - tail), BF16)
        w[:, tail:V] = b.w_in[:, tail:V]
    got_q()
    q_rows = b.q_all[...].reshape(R, HD)
    s = dot(q_rows, k[...], 1, 1) * scale
    place = lax.broadcasted_iota(jnp.int32, (R, KJ), 1) + ms * KJ
    s = jnp.where(place < ln[0], s, -jnp.inf)
    b.s[...] = s
    peak = jnp.maximum(jnp.max(s, axis=1, keepdims=True), -1e30)
    e = jnp.exp(s - peak)
    total = jnp.sum(e, axis=1, keepdims=True)
    acc = dot(e.astype(BF16), v[...], 1, 0) / jnp.maximum(total, 1e-30)
    b.acc_send[...] = acc.astype(BF16).reshape(NS, TR, HD)
    b.st_send[...] = lane_pick(peak, total, R).reshape(NS, TR, 128)
    got_st = scatter(b.st_send, b.st_recv, "seq")
    got_acc = scatter(b.acc_send, b.acc_recv, "seq")
    got_st()
    tiles = [b.st_send[ms]] + [b.st_recv[i] for i in range(NS - 1)]
    peaks = [t[:, 0:1] for t in tiles]
    totals = [t[:, 64:65] for t in tiles]
    top = functools.reduce(jnp.maximum, peaks)
    parts = [t * jnp.exp(p - top) for t, p in zip(totals, peaks)]
    whole = functools.reduce(jnp.add, parts)
    got_acc()
    accs = [b.acc_send[ms]] + [b.acc_recv[i] for i in range(NS - 1)]
    att = functools.reduce(jnp.add, [a.astype(F32) * (p / whole) for a, p in zip(accs, parts)])
    b.att_all[ms] = att.astype(BF16)
    b.stat_all[ms] = lane_pick(top, whole, TR)
    got_att = spread(b.att_all.at[ms], b.att_all, "seq")
    got_stat = spread(b.stat_all.at[ms], b.stat_all, "seq")
    got_att()

    mixed_part = dot(b.att_all[...].reshape(R, HD), wo[...], 1, 0)
    b.mix_send[...] = mixed_part.astype(BF16).reshape(NV, RB, C)
    got_mix = scatter(b.mix_send, b.mix_recv, "vocab")
    mine = res[pl.ds(pl.multiple_of(mv * RB, RB), RB), :].astype(F32)
    got_mix()
    mixed = mine + b.mix_send[mv].astype(F32)
    for i in range(NV - 1):
        mixed = mixed + b.mix_recv[i].astype(F32)
    b.mixed[...] = mixed
    b.mg[mv] = (mixed * gain[...]).astype(BF16)
    got_mg = spread(b.mg.at[mv], b.mg, "vocab")
    b.sq[ms] = sub_pick([to_row(jnp.sum(mixed * mixed, axis=1, keepdims=True), RB)])
    got_sq = spread(b.sq.at[ms], b.sq, "seq")
    got_sq()
    square = jnp.sum(b.sq[...], axis=0)[0:1]
    b.inv[mv] = sub_pick([lax.rsqrt(square / D + EPS)])
    got_inv = spread(b.inv.at[mv], b.inv, "vocab")
    got_mg()

    def rows_of(owner):
        return b.mg[pl.ds(owner * NB, NB)].reshape(TR, C)

    def at(distance):
        return lax.rem(ms + distance + NS, NS)

    half = [slice(0, VH), slice(VH, VP)]
    cw_send, cw_recv, cc_send, cc_recv = b.cw_send, b.cw_recv, b.cc_send, b.cc_recv
    cw_got, cc_got = {}, {}
    far = rows_of(at(H))
    for hh in range(2):
        block = dot(far, w[:, half[hh]], 1, 0)
        if hh == 0:
            cw_send[0, 0] = block
            cw_got[0, 0] = one(cw_send.at[0, 0], cw_recv.at[0, 0], "seq", right)
        else:
            cc_send[0, 1] = block
            cc_got[0, 1] = one(cc_send.at[0, 1], cc_recv.at[0, 1], "seq", left)
    for step in range(1, H):
        both = jnp.concatenate([rows_of(at(H - step)), rows_of(at(step - H))], axis=0)
        for hh in range(2):
            block = dot(both, w[:, half[hh]], 1, 0)
            cw_send[step, hh] = block[:TR]
            cc_send[step, hh] = block[TR:]
        for hh in range(2):
            for way in ((0, 1) if hh == 0 else (1, 0)):
                sends, recvs, got, to = ((cw_send, cw_recv, cw_got, right), (cc_send, cc_recv, cc_got, left))[way]
                if (step - 1, hh) in got:
                    got[step - 1, hh]()
                    sends[step, hh] = sends[step, hh] + recvs[step - 1, hh]
                got[step, hh] = one(sends.at[step, hh], recvs.at[step, hh], "seq", to)
    own = rows_of(ms)
    for hh in range(2):
        b.logits[:, half[hh]] = dot(own, w[:, half[hh]], 1, 0)
    got_inv()
    normed = []
    for i in range(NV):
        normed.append(b.mg[i].astype(F32) * to_col(b.inv[i][0:1], RB))
    b.normed_t[...] = jnp.transpose(jnp.concatenate(normed, axis=0)).astype(BF16)
    inv_own = jnp.concatenate([to_col(b.inv[ms * NB + i][0:1], RB) for i in range(NB)], axis=0)
    for hh in range(2):
        block = b.logits[:, half[hh]]
        for got, recvs in ((cw_got, cw_recv), (cc_got, cc_recv)):
            if (H - 1, hh) in got:
                got[H - 1, hh]()
                block = block + recvs[H - 1, hh]
        block = block * inv_own
        if hh == 1:
            col = lax.broadcasted_iota(jnp.int32, (TR, VH), 1) + VH
            block = jnp.where(col < V, block, -jnp.inf)
        b.logits[:, half[hh]] = block

    logits = b.logits[...]
    tgt_col = to_col(jnp.concatenate([tgt[...].astype(F32), jnp.zeros((1, 128 - TR), F32)], axis=1), TR)
    tgt_col = tgt_col.astype(jnp.int32) - mv * V
    col = lax.broadcasted_iota(jnp.int32, (TR, VP), 1)
    hit = jnp.logical_and(col == tgt_col, col < V)
    row_peak = jnp.max(logits, axis=1, keepdims=True)
    row_sum = jnp.sum(jnp.exp(logits - row_peak), axis=1, keepdims=True)
    row_tgt = jnp.sum(jnp.where(hit, logits, 0.0), axis=1, keepdims=True)
    b.stats[mv] = sub_pick([to_row(x, TR) for x in (row_peak, row_sum, row_tgt)])
    got_stats = spread(b.stats.at[mv], b.stats, "vocab")
    got_stats()
    st = b.stats[...]
    tops = jnp.max(st[:, 0:1, :], axis=0)
    sums = jnp.sum(st[:, 1:2, :] * jnp.exp(st[:, 0:1, :] - tops[None]), axis=0)
    hits = jnp.sum(st[:, 2:3, :], axis=0)
    log_total = tops + jnp.log(sums)
    loss = log_total - hits + ZW * log_total * log_total
    lane = lax.broadcasted_iota(jnp.int32, (1, 128), 1)
    loss = jnp.where(lane < TR, loss, 0.0)
    lt = to_col(jnp.where(lane < TR, log_total, 0.0), TR)
    grad = jnp.exp(logits - lt) * (1.0 + 2.0 * ZW * lt) - hit.astype(F32)
    grad = grad.astype(BF16)
    g_all = b.g_all
    for hh in range(2):
        g_all[ms, hh] = grad[:, half[hh]]

    cw_got, cc_got = {}, {}

    def forward(step, hh, way):
        if step == H - 1 and hh != way:
            return
        got, to, owner = ((cw_got, right, at(-step)), (cc_got, left, at(step)))[way]
        if step > 0:
            got[step - 1, hh]()
        got[step, hh] = one(g_all.at[owner, hh], g_all.at[owner, hh], "seq", to)

    def hidden(owners):
        out = None
        for hh in range(2):
            rows = jnp.concatenate([g_all[o, hh] for o in owners], axis=0)
            term = dot(rows, w[:, half[hh]], 1, 1)
            out = term if out is None else out + term
        out = out.astype(BF16)
        for i, o in enumerate(owners):
            b.hid_send[pl.ds(o * NB, NB)] = out[i * TR:(i + 1) * TR].reshape(NB, RB, C)

    for step in range(H):
        for hh in range(2):
            for way in range(2):
                forward(step, hh, way)
        if step == 0:
            b.loss[ms] = sub_pick([loss])
            got_loss = spread(b.loss.at[ms], b.loss, "seq")
            hidden([ms])
        else:
            for got in (cw_got, cc_got):
                for hh in range(2):
                    if step == H - 1 and (step, hh) not in got:
                        got[step - 1, hh]()
            hidden([at(-step), at(step)])
    cw_got[H - 1, 0]()
    cc_got[H - 1, 1]()
    hidden([at(H)])
    got_hid = scatter(b.hid_send, b.hid_recv, "vocab")

    QC = C // 4

    def head(start, size):
        rows = b.normed_t[pl.ds(pl.multiple_of(start, QC), size), :]
        return [dot(rows, g_all[:, hh].reshape(R, VH), 1, 0).astype(BF16) for hh in range(2)]

    hp = 1 - core
    for i in range(2):
        for hh, block in enumerate(head((2 * hp + i) * QC, QC)):
            b.hg_send[i, :, half[hh]] = block
    got_h1 = one(b.hg_send, b.hg_recv, "dp", mate)

    got_hid()
    normed_grad = b.hid_send[mv].astype(F32)
    for i in range(NV - 1):
        normed_grad = normed_grad + b.hid_recv[i].astype(F32)
    gated = normed_grad * gain[...]
    mixed = b.mixed[...]
    b.dots[ms] = sub_pick([to_row(jnp.sum(gated * mixed, axis=1, keepdims=True), RB)])
    got_dots = spread(b.dots.at[ms], b.dots, "seq")
    for i in range(2):
        for hh, block in enumerate(head((2 * core + i) * QC, QC)):
            b.hg_own[i, :, half[hh]] = block
    got_loss()
    b.loss1[0] = jnp.sum(b.loss[...], axis=0)
    got_l1 = one(b.loss1.at[0], b.loss1.at[1], "dp", mate)
    got_dots()
    dots = to_col(jnp.sum(b.dots[...], axis=0)[0:1], RB)
    inv = to_col(b.inv[mv][0:1], RB)
    mixed_grad = gated * inv - mixed * (inv * inv * inv * dots / D)
    b.mgrad[mv] = mixed_grad.astype(BF16)
    got_mgrad = spread(b.mgrad.at[mv], b.mgrad, "vocab")

    got_h1()
    zq = 1 - zlo
    b.q_send[...] = (b.hg_own[zq].astype(F32) + b.hg_recv[zq].astype(F32)).astype(BF16)
    got_h2 = one(b.q_send, b.q_recv, "dp", zmate)
    got_l1()
    b.loss2[0] = b.loss1[0] + b.loss1[1]
    got_l2 = one(b.loss2.at[0], b.loss2.at[1], "dp", zmate)

    got_mgrad()
    ag_part = dot(b.mgrad[...].reshape(R, C), wo[...], 1, 1)
    b.ag_send[...] = ag_part.astype(BF16).reshape(NS, TR, HD)
    got_ag = scatter(b.ag_send, b.ag_recv, "seq")
    got_stat()
    stat = b.stat_all[...].reshape(R, 128)
    weights = jnp.exp(b.s[...] - stat[:, 0:1]) / stat[:, 64:65]
    weights_half = weights.astype(BF16)
    got_ag()
    ag = b.ag_send[ms].astype(F32)
    for i in range(NS - 1):
        ag = ag + b.ag_recv[i].astype(F32)
    b.ag_all[ms] = ag.astype(BF16)
    got_ag_all = spread(b.ag_all.at[ms], b.ag_all, "seq")
    got_ag_all()
    ag_rows = b.ag_all[...].reshape(R, HD)
    prob_grad = dot(ag_rows, v[...], 1, 1)
    delta = jnp.sum(weights * prob_grad, axis=1, keepdims=True)
    step = min(R, 128)
    for i in range(R // step):
        b.delta[ms, i] = sub_pick([to_row(delta[i * step:(i + 1) * step], step)])
    got_delta = spread(b.delta.at[ms], b.delta, "seq")
    out_vg[...] = dot(weights_half, ag_rows, 0, 0)
    got_delta()
    deltas = jnp.sum(b.delta[...], axis=0)
    delta = jnp.concatenate([to_col(deltas[i, 0:1], step) for i in range(R // step)], axis=0)
    score_grad = (weights * (prob_grad - delta) * scale).astype(BF16)
    out_kg[...] = dot(score_grad, b.q_all[...].reshape(R, HD), 0, 0)

    got_h2()
    fin = b.fin
    mine_at = 2 * core + zlo
    fin[mine_at] = (
        b.hg_own[zlo].astype(F32) + b.hg_recv[zlo].astype(F32) + b.q_recv[...].astype(F32)
    ).astype(BF16)
    got_f1 = one(fin.at[mine_at], fin.at[mine_at], "dp", zmate)
    got_f2 = one(fin.at[mine_at], fin.at[mine_at], "dp", mate)
    got_l2()
    loss = (b.loss2[0] + b.loss2[1])[0:1]
    out_loss[...] = jnp.sum(loss, axis=1, keepdims=True) / batch_rows
    got_f1()
    other_at = 2 * core + zq
    got_f3 = one(fin.at[other_at], fin.at[other_at], "dp", mate)
    got_f2()
    got_f3()
    store = pltpu.make_async_copy(fin, out_hg, b.lsem.at[1])
    store.start()
    for item in drains:
        if isinstance(item, tuple):
            wait_bytes(*item)
        else:
            item.wait_send()
    store.wait()


def scratch_list(cfg):
    NS, NV, TR, KJ, C, V, VP, batch_rows = cfg
    HD = HDIM
    R = TR * NS
    RB = R // NV
    H = NS // 2
    VH = VP // 2
    blocks = max(1, R // 128)

    def vm(*shape, dtype=BF16):
        return pltpu.VMEM(shape, dtype)

    return dict(
        w_in=vm(C, V), w=vm(C, VP),
        q_all=vm(NS, TR, HD), s=vm(R, KJ, dtype=F32),
        acc_send=vm(NS, TR, HD), acc_recv=vm(NS, TR, HD),
        st_send=vm(NS, TR, 128, dtype=F32), st_recv=vm(NS, TR, 128, dtype=F32),
        att_all=vm(NS, TR, HD), stat_all=vm(NS, TR, 128, dtype=F32),
        mix_send=vm(NV, RB, C), mix_recv=vm(NV, RB, C), mixed=vm(RB, C, dtype=F32),
        mg=vm(NV, RB, C), sq=vm(NS, 8, 128, dtype=F32), inv=vm(NV, 8, 128, dtype=F32),
        cw_send=vm(H, 2, TR, VH, dtype=F32), cw_recv=vm(H, 2, TR, VH, dtype=F32),
        cc_send=vm(H, 2, TR, VH, dtype=F32), cc_recv=vm(H, 2, TR, VH, dtype=F32),
        logits=vm(TR, VP, dtype=F32), stats=vm(NV, 8, 128, dtype=F32),
        normed_t=vm(C, R), g_all=vm(NS, 2, TR, VH),
        loss=vm(NS, 8, 128, dtype=F32), loss1=vm(2, 8, 128, dtype=F32),
        loss2=vm(2, 8, 128, dtype=F32),
        hid_send=vm(NV, RB, C), hid_recv=vm(NV, RB, C), dots=vm(NS, 8, 128, dtype=F32),
        mgrad=vm(NV, RB, C), ag_send=vm(NS, TR, HD), ag_recv=vm(NS, TR, HD),
        ag_all=vm(NS, TR, HD), delta=vm(NS, blocks, 8, 128, dtype=F32),
        hg_send=vm(2, C // 4, VP), hg_recv=vm(2, C // 4, VP), hg_own=vm(2, C // 4, VP),
        q_send=vm(C // 4, VP), q_recv=vm(C // 4, VP), fin=vm(4, C // 4, VP),
        ssem=pltpu.SemaphoreType.DMA((80,)), rsem=pltpu.SemaphoreType.DMA((80,)),
        lsem=pltpu.SemaphoreType.DMA((2,)),
    )


def body(sizes, queries, enc_keys, enc_values, enc_lengths, out_proj, residual, norm_gain, head_weight, targets):
    ND, NS, NV = sizes
    TR = queries.shape[1]
    KJ = enc_keys.shape[1]
    C, V = head_weight.shape
    VP = (V + 255) // 256 * 256
    cfg = (NS, NV, TR, KJ, C, V, VP, ND * TR * NS)
    vmem = pl.BlockSpec(memory_space=pltpu.VMEM)
    call = pl.pallas_call(
        functools.partial(kernel, cfg),
        out_shape=(
            jax.ShapeDtypeStruct((1, 1), F32),
            jax.ShapeDtypeStruct((4, C // 4, VP), BF16),
            jax.ShapeDtypeStruct((KJ, HDIM), F32),
            jax.ShapeDtypeStruct((KJ, HDIM), F32),
        ),
        in_specs=[vmem, vmem, vmem, pl.BlockSpec(memory_space=pltpu.SMEM), vmem, vmem, vmem,
                  pl.BlockSpec(memory_space=pl.ANY), vmem],
        out_specs=(vmem, pl.BlockSpec(memory_space=pl.ANY), vmem, vmem),
        scratch_shapes=list(scratch_list(cfg).values()),
        compiler_params=pltpu.CompilerParams(
            collective_id=0, has_side_effects=True, vmem_limit_bytes=48 * 1024 * 1024),
    )
    loss, hg, kg, vg = call(
        queries[0], enc_keys[0], enc_values[0], enc_lengths, out_proj, residual[0],
        norm_gain.reshape(1, C), head_weight, targets)
    return (loss.reshape(()), hg.reshape(C, VP)[:, :V], kg[None], vg[None])


def solution(mesh):
    placed = (
        P("dp", "seq", "vocab"),
        P("dp", "seq", "vocab"),
        P("dp", "seq", "vocab"),
        P("dp"),
        P("vocab", "seq"),
        P("dp", None, "seq"),
        P("seq"),
        P("seq", "vocab"),
        P("dp", "seq"),
    )
    sizes = (mesh.shape["dp"], mesh.shape["seq"], mesh.shape["vocab"])
    return jax.shard_map(
        functools.partial(body, sizes),
        mesh=mesh,
        in_specs=placed,
        out_specs=(P(), P("seq", "vocab"), P("dp", "seq", "vocab"), P("dp", "seq", "vocab")),
        check_vma=False,
    )
```

```python
import functools
import types

import jax
import jax.numpy as jnp
from jax import lax
from jax.experimental import pallas as pl
from jax.experimental.pallas import tpu as pltpu
from jax.sharding import PartitionSpec as P

HDIM = 256
ZW = 0.0001
EPS = 1e-06
MESH = pl.DeviceIdType.MESH
F32 = jnp.float32
BF16 = jnp.bfloat16


def dot(a, b, ca, cb):
    return lax.dot_general(a, b, (((ca,), (cb,)), ((), ())), preferred_element_type=F32)


def eye(n, m):
    return lax.broadcasted_iota(jnp.int32, (n, m), 0) == lax.broadcasted_iota(jnp.int32, (n, m), 1)


def to_row(col, n):
    return jnp.sum(jnp.where(eye(n, 128), jnp.broadcast_to(col, (n, 128)), 0.0), axis=0, keepdims=True)


def to_col(row, n):
    return jnp.sum(jnp.where(eye(n, 128), jnp.broadcast_to(row, (n, 128)), 0.0), axis=1, keepdims=True)


def sub_pick(rows):
    sub = lax.broadcasted_iota(jnp.int32, (8, 128), 0)
    tile = jnp.zeros((8, 128), F32)
    for i, row in enumerate(rows):
        tile = jnp.where(sub == i, row, tile)
    return tile


def kernel(cfg, q_hbm, k_hbm, v_hbm, ln, wo_hbm, res_hbm, gain_hbm, w_hbm, tgt_hbm, out_loss, out_hg, out_kg, out_vg, *scratch):
    NS, NV, TR, KJ, C, V, VP, batch_rows = cfg
    b = types.SimpleNamespace(**dict(zip(scratch_list(cfg), scratch)))
    HD = HDIM
    R = TR * NS
    RB = R // NV
    NB = TR // RB
    H = NS // 2
    VH = VP // 2
    D = C * NS
    scale = HD ** (-0.5)
    md, ms, mv = lax.axis_index("dp"), lax.axis_index("seq"), lax.axis_index("vocab")
    core = lax.rem(md, 2)
    zlo = md // 2
    mate = md + 1 - 2 * core
    zmate = lax.rem(md + 2, 4)
    right, left = lax.rem(ms + 1, NS), lax.rem(ms + NS - 1, NS)
    ssem, rsem = b.ssem, b.rsem
    used = [0]

    def sem():
        used[0] += 1
        return ssem.at[used[0] - 1], rsem.at[used[0] - 1]

    def push(src, dst, axis, to, sems):
        copy = pltpu.make_async_remote_copy(
            src_ref=src, dst_ref=dst, send_sem=sems[0], recv_sem=sems[1],
            device_id={axis: to}, device_id_type=MESH)
        copy.start()
        return copy

    drains = []

    def wait_bytes(ref, one):
        pltpu.make_async_copy(ref, ref, one).wait()

    NX = min(4, NV)
    NZ = NV // NX
    vx, vz = lax.rem(mv, NX), mv // NX
    seq_steps = sorted(range(1, NS), key=lambda a: -min(a, NS - a))
    vocab_steps = sorted(
        [(a, c) for a in range(NZ) for c in range(NX) if a or c],
        key=lambda d: -(2 * min(d[0], NZ - d[0]) + min(d[1], NX - d[1])))

    def others(axis):
        if axis == "seq":
            return [lax.rem(ms + a, NS) for a in seq_steps]
        return [lax.rem(vz + a, NZ) * NX + lax.rem(vx + c, NX) for a, c in vocab_steps]

    def spread(src, dst, axis):
        me, n = (ms, NS) if axis == "seq" else (mv, NV)
        sems = sem()
        for to in others(axis):
            push(src, dst.at[me], axis, to, sems)
        rest = dst.at[pl.ds(0, n - 1)]
        drains.append((rest, sems[0]))
        return lambda: wait_bytes(rest, sems[1])

    def scatter(src, dst, axis):
        n = NS if axis == "seq" else NV
        sems = sem()
        for i, to in enumerate(others(axis)):
            push(src.at[to], dst.at[i], axis, to, sems)
        rest = dst.at[pl.ds(0, n - 1)]
        drains.append((rest, sems[0]))
        return lambda: wait_bytes(rest, sems[1])

    def one(src, dst, axis, to):
        copy = push(src, dst, axis, to, sem())
        drains.append(copy)
        return copy.wait_recv

    barrier = pltpu.get_barrier_semaphore()
    for step in range(1, NS):
        pl.semaphore_signal(barrier, inc=1, device_id={"seq": lax.rem(ms + step, NS)}, device_id_type=MESH)
    for step in range(1, NV):
        pl.semaphore_signal(barrier, inc=1, device_id={"vocab": lax.rem(mv + step, NV)}, device_id_type=MESH)
    for to in (mate, zmate):
        pl.semaphore_signal(barrier, inc=1, device_id={"dp": to}, device_id_type=MESH)
    w = b.w
    k, v, wo, res, gain, tgt = b.k, b.v, b.wo, b.res, b.gain, b.tgt
    loads = []
    for i, (src, dst) in enumerate(
        ((q_hbm, b.q_all.at[ms]), (k_hbm, k), (v_hbm, v), (wo_hbm, wo), (res_hbm, res), (gain_hbm, gain),
         (tgt_hbm, tgt), (w_hbm, w.at[pl.ds(0, V)]))
    ):
        loads.append(pltpu.make_async_copy(src, dst, b.lsem.at[i]))
        loads[-1].start()
    pl.semaphore_wait(barrier, NS - 1 + NV - 1 + 2)

    got_q = spread(q_hbm, b.q_all, "seq")
    for load in loads[:3]:
        load.wait()
    got_q()
    q_rows = b.q_all[...].reshape(R, HD)
    s = dot(q_rows, k[...], 1, 1) * scale
    place = lax.broadcasted_iota(jnp.int32, (R, KJ), 1) + ms * KJ
    s = jnp.where(place < ln[0], s, -jnp.inf)
    b.s[...] = s
    peak = jnp.maximum(jnp.max(s, axis=1, keepdims=True), -1e30)
    e = jnp.exp(s - peak)
    total = jnp.sum(e, axis=1, keepdims=True)
    denom = jnp.maximum(total, 1e-30)
    e_top = e.astype(BF16)
    e_rest = e - e_top.astype(F32)
    e_mid = e_rest.astype(BF16)
    e_low = (e_rest - e_mid.astype(F32)).astype(BF16)
    acc = dot(e_top, v[...], 1, 0)
    b.acc_send[...] = (acc / denom).astype(BF16).reshape(NS, TR, HD)
    for i in range(NS):
        rows = slice(i * TR, (i + 1) * TR)
        b.st_send[i] = sub_pick([to_row(peak[rows], TR), to_row(total[rows], TR)])
    got_st = scatter(b.st_send, b.st_recv, "seq")
    got_acc = scatter(b.acc_send, b.acc_recv, "seq")
    acc = acc + (dot(e_mid, v[...], 1, 0) + dot(e_low, v[...], 1, 0))
    b.full_send[...] = (acc / denom).reshape(NS, TR, HD)
    for load in loads[3:]:
        load.wait()
    if V < VP:
        w[V:VP] = jnp.zeros((VP - V, C), BF16)
    got_st()
    b.st_recv[NS - 1] = b.st_send[ms]
    tiles = b.st_recv[...]
    top = jnp.max(tiles[:, 0:1], axis=0)
    parts = tiles[:, 1:2] * jnp.exp(tiles[:, 0:1] - top[None])
    whole = jnp.sum(parts, axis=0)
    shares = [to_col(parts[i] / whole, TR) for i in range(NS)]
    b.stat_all[ms] = sub_pick([top, whole])
    got_acc()
    att = b.acc_send[ms].astype(F32) * shares[NS - 1]
    for i in range(NS - 1):
        att = att + b.acc_recv[i].astype(F32) * shares[i]
    b.att_all[ms] = att.astype(BF16)
    got_att = spread(b.att_all.at[ms], b.att_all, "seq")
    got_stat = spread(b.stat_all.at[ms], b.stat_all, "seq")
    got_full = scatter(b.full_send, b.full_recv, "seq")
    got_att()

    mixed_part = dot(b.att_all[...].reshape(R, HD), wo[...], 1, 0)
    b.mix_send[...] = mixed_part.astype(BF16).reshape(NV, RB, C)
    got_mix = scatter(b.mix_send, b.mix_recv, "vocab")
    mine = res[pl.ds(pl.multiple_of(mv * RB, RB), RB), :].astype(F32)
    got_mix()
    mixed = mine + b.mix_send[mv].astype(F32)
    for i in range(NV - 1):
        mixed = mixed + b.mix_recv[i].astype(F32)
    b.mixed[...] = mixed
    b.mg[mv] = (mixed * gain[...]).astype(BF16)
    got_mg = spread(b.mg.at[mv], b.mg, "vocab")
    b.sq[ms] = sub_pick([to_row(jnp.sum(mixed * mixed, axis=1, keepdims=True), RB)])
    got_sq = spread(b.sq.at[ms], b.sq, "seq")
    got_sq()
    square = jnp.sum(b.sq[...], axis=0)[0:1]
    b.inv[mv] = sub_pick([lax.rsqrt(square / D + EPS)])
    got_inv = spread(b.inv.at[mv], b.inv, "vocab")
    got_mg()

    def rows_of(owner):
        return b.mg[pl.ds(owner * NB, NB)].reshape(TR, C)

    def at(distance):
        return lax.rem(ms + distance + NS, NS)

    half = [slice(0, VH), slice(VH, VP)]
    cw_send, cw_recv, cc_send, cc_recv = b.cw_send, b.cw_recv, b.cc_send, b.cc_recv
    cw_got, cc_got = {}, {}
    far = rows_of(at(H))
    for hh in range(2):
        block = dot(far, w[half[hh]], 1, 1)
        if hh == 0:
            cw_send[0, 0] = block
            cw_got[0, 0] = one(cw_send.at[0, 0], cw_recv.at[0, 0], "seq", right)
        else:
            cc_send[0, 1] = block
            cc_got[0, 1] = one(cc_send.at[0, 1], cc_recv.at[0, 1], "seq", left)
    for step in range(1, H):
        both = jnp.concatenate([rows_of(at(H - step)), rows_of(at(step - H))], axis=0)
        for hh in range(2):
            block = dot(both, w[half[hh]], 1, 1)
            cw_send[step, hh] = block[:TR]
            cc_send[step, hh] = block[TR:]
        for hh in range(2):
            for way in ((0, 1) if hh == 0 else (1, 0)):
                sends, recvs, got, to = ((cw_send, cw_recv, cw_got, right), (cc_send, cc_recv, cc_got, left))[way]
                if (step - 1, hh) in got:
                    got[step - 1, hh]()
                    sends[step, hh] = sends[step, hh] + recvs[step - 1, hh]
                got[step, hh] = one(sends.at[step, hh], recvs.at[step, hh], "seq", to)
    own = rows_of(ms)
    for hh in range(2):
        b.logits[:, half[hh]] = dot(own, w[half[hh]], 1, 1)
    got_full()
    att_full = b.full_send[ms] * shares[NS - 1]
    for i in range(NS - 1):
        att_full = att_full + b.full_recv[i] * shares[i]
    b.att_full[...] = att_full
    got_inv()
    normed = []
    for i in range(NV):
        normed.append(b.mg[i].astype(F32) * to_col(b.inv[i][0:1], RB))
    b.normed[...] = jnp.concatenate(normed, axis=0).astype(BF16)
    inv_own = jnp.concatenate([to_col(b.inv[ms * NB + i][0:1], RB) for i in range(NB)], axis=0)
    for hh in range(2):
        block = b.logits[:, half[hh]]
        for got, recvs in ((cw_got, cw_recv), (cc_got, cc_recv)):
            if (H - 1, hh) in got:
                got[H - 1, hh]()
                block = block + recvs[H - 1, hh]
        block = block * inv_own
        if hh == 1:
            col = lax.broadcasted_iota(jnp.int32, (TR, VH), 1) + VH
            block = jnp.where(col < V, block, -jnp.inf)
        b.logits[:, half[hh]] = block

    logits = b.logits[...]
    tgt_col = to_col(jnp.concatenate([tgt[...].astype(F32), jnp.zeros((1, 128 - TR), F32)], axis=1), TR)
    tgt_col = tgt_col.astype(jnp.int32) - mv * V
    col = lax.broadcasted_iota(jnp.int32, (TR, VP), 1)
    hit = jnp.logical_and(col == tgt_col, col < V)
    row_peak = jnp.max(logits, axis=1, keepdims=True)
    row_sum = jnp.sum(jnp.exp(logits - row_peak), axis=1, keepdims=True)
    row_tgt = jnp.sum(jnp.where(hit, logits, 0.0), axis=1, keepdims=True)
    b.stats[mv] = sub_pick([to_row(x, TR) for x in (row_peak, row_sum, row_tgt)])
    got_stats = spread(b.stats.at[mv], b.stats, "vocab")
    got_stats()
    st = b.stats[...]
    tops = jnp.max(st[:, 0:1, :], axis=0)
    sums = jnp.sum(st[:, 1:2, :] * jnp.exp(st[:, 0:1, :] - tops[None]), axis=0)
    hits = jnp.sum(st[:, 2:3, :], axis=0)
    log_total = tops + jnp.log(sums)
    loss = log_total - hits + ZW * log_total * log_total
    lane = lax.broadcasted_iota(jnp.int32, (1, 128), 1)
    loss = jnp.where(lane < TR, loss, 0.0)
    lt = to_col(jnp.where(lane < TR, log_total, 0.0), TR)
    grad = jnp.exp(logits - lt) * (1.0 + 2.0 * ZW * lt) - hit.astype(F32)
    grad = grad.astype(BF16)
    g_all = b.g_all
    VQ = VP // 4
    along = jnp.sum(jnp.where(col < V, grad.astype(F32) * logits, 0.0), axis=1, keepdims=True)
    b.along[mv] = sub_pick([to_row(along, TR)])
    for i in range(4):
        g_all[ms, i] = grad[:, i * VQ:(i + 1) * VQ]

    cw_got, cc_got = {}, {}

    def forward(step, hh, way):
        if step == H - 1 and hh != way:
            return
        got, to, owner = ((cw_got, right, at(-step)), (cc_got, left, at(step)))[way]
        if step > 0:
            got[step - 1, hh]()
        piece = g_all.at[owner, pl.ds(2 * hh, 2)]
        got[step, hh] = one(piece, piece, "seq", to)

    hid_sems = sem()
    b_hid = b.hid_recv

    def hidden(owners):
        out = None
        for i in range(4):
            rows = jnp.concatenate([g_all[o, i] for o in owners], axis=0)
            term = dot(rows, w[i * VQ:(i + 1) * VQ], 1, 0)
            out = term if out is None else out + term
        out = out.astype(BF16)
        for i, o in enumerate(owners):
            b.hid_send[pl.ds(o * NB, NB)] = out[i * TR:(i + 1) * TR].reshape(NB, RB, C)
            for part in range(NB):
                to = o * NB + part

                @pl.when(to != mv)
                def _():
                    push(b.hid_send.at[to], b_hid.at[mv], "vocab", to, hid_sems)

    for step in range(H):
        for hh in range(2):
            for way in range(2):
                forward(step, hh, way)
        if step == 0:
            got_along = spread(b.along.at[mv], b.along, "vocab")
            hidden([ms])
        else:
            for got in (cw_got, cc_got):
                for hh in range(2):
                    if step == H - 1 and (step, hh) not in got:
                        got[step - 1, hh]()
            hidden([at(-step), at(step)])
        if step == min(1, H - 1):
            got_along()
            b.loss[ms] = sub_pick([loss, jnp.sum(b.along[...], axis=0)[0:1]])
            got_loss = spread(b.loss.at[ms], b.loss, "seq")
    cw_got[H - 1, 0]()
    cc_got[H - 1, 1]()
    hidden([at(H)])

    def head(quarter):
        return dot(g_all[:, quarter].reshape(R, VQ), b.normed[...], 0, 0).astype(BF16)

    got_half = []
    for i in range(2):
        b.hg_send[i] = head(2 * (1 - core) + i)
        got_half.append(one(b.hg_send.at[i], b.hg_recv.at[i], "dp", mate))
    for i in range(2):
        b.hg_own[i] = head(2 * core + i)
    got_pair = []
    for i in range(2):
        got_half[i]()
        b.hg_pair[i] = (b.hg_own[i].astype(F32) + b.hg_recv[i].astype(F32)).astype(BF16)
        got_pair.append(one(b.hg_pair.at[i], b.hg_far.at[i], "dp", zmate))

    rest = b_hid.at[pl.ds(0, NV - 1)]
    drains.append((rest, hid_sems[0]))
    wait_bytes(rest, hid_sems[1])
    b_hid[mv] = b.hid_send[mv]
    gated = jnp.sum(b_hid[...].astype(F32), axis=0) * gain[...]
    got_loss()
    b.loss1[0] = jnp.sum(b.loss[...], axis=0)
    got_l1 = one(b.loss1.at[0], b.loss1.at[1], "dp", mate)
    row = lax.broadcasted_iota(jnp.int32, (RB, 128), 0) + lax.rem(mv, NB) * RB
    lane = lax.broadcasted_iota(jnp.int32, (RB, 128), 1)
    tile = jnp.broadcast_to(b.loss[mv // NB][1:2], (RB, 128))
    along = jnp.sum(jnp.where(row == lane, tile, 0.0), axis=1, keepdims=True)
    inv = to_col(b.inv[mv][0:1], RB)
    mixed_grad = gated * inv - b.mixed[...] * (inv * inv * along / D)
    b.mgrad[mv] = mixed_grad.astype(BF16)
    got_mgrad = spread(b.mgrad.at[mv], b.mgrad, "vocab")
    got_l1()
    b.loss2[0] = b.loss1[0] + b.loss1[1]
    got_l2 = one(b.loss2.at[0], b.loss2.at[1], "dp", zmate)
    got_stat()
    tops = jnp.concatenate([to_col(b.stat_all[i][0:1], TR) for i in range(NS)], axis=0)
    sums = jnp.concatenate([to_col(b.stat_all[i][1:2], TR) for i in range(NS)], axis=0)
    weights = jnp.exp(b.s[...] - tops) / sums
    b.s[...] = weights

    got_mgrad()
    ag_part = dot(b.mgrad[...].reshape(R, C), wo[...], 1, 1)
    b.ag_send[...] = ag_part.astype(BF16).reshape(NS, TR, HD)
    got_ag = scatter(b.ag_send, b.ag_recv, "seq")
    got_ag()
    ag = b.ag_send[ms].astype(F32)
    for i in range(NS - 1):
        ag = ag + b.ag_recv[i].astype(F32)
    ag = ag.astype(BF16)
    b.ag_all[ms] = ag
    got_ag_all = spread(b.ag_all.at[ms], b.ag_all, "seq")
    delta = jnp.sum(ag.astype(F32) * b.att_full[...], axis=1, keepdims=True)
    b.delta[ms] = sub_pick([to_row(delta, TR)])
    got_delta = spread(b.delta.at[ms], b.delta, "seq")
    fin = b.fin

    def finish_half(i):
        got_pair[i]()
        fin[2 * core + i] = (b.hg_pair[i].astype(F32) + b.hg_far[i].astype(F32)).astype(BF16)
        piece = fin.at[2 * core + i]
        return one(piece, piece, "dp", mate)

    got_fin = [finish_half(0)]
    got_ag_all()
    got_delta()
    ag_rows = b.ag_all[...].reshape(R, HD)
    prob_grad = dot(ag_rows, v[...], 1, 1)
    delta = jnp.concatenate([to_col(b.delta[i][0:1], TR) for i in range(NS)], axis=0)
    weights = b.s[...]
    score_grad = (weights * (prob_grad - delta) * scale).astype(BF16)
    b.kg[...] = dot(score_grad, b.q_all[...].reshape(R, HD), 0, 0)
    b.vg[...] = dot(weights.astype(BF16), ag_rows, 0, 0)
    stores = []
    for i, (src, dst) in enumerate(((b.kg, out_kg), (b.vg, out_vg))):
        stores.append(pltpu.make_async_copy(src, dst, b.lsem.at[12 + i]))
        stores[-1].start()
    got_l2()
    loss = (b.loss2[0] + b.loss2[1])[0:1]
    out_loss[...] = jnp.sum(loss, axis=1, keepdims=True) / batch_rows
    got_fin.append(finish_half(1))
    for got in got_fin:
        got()
    for i in range(4):
        size = min(VQ, V - i * VQ)
        if size > 0:
            store = pltpu.make_async_copy(fin.at[i, pl.ds(0, size)], out_hg.at[pl.ds(i * VQ, size)], b.lsem.at[8 + i])
            store.start()
            stores.append(store)
    for item in drains:
        if isinstance(item, tuple):
            wait_bytes(*item)
        else:
            item.wait_send()
    for store in stores:
        store.wait()


def scratch_list(cfg):
    NS, NV, TR, KJ, C, V, VP, batch_rows = cfg
    HD = HDIM
    R = TR * NS
    RB = R // NV
    H = NS // 2
    VH = VP // 2

    def vm(*shape, dtype=BF16):
        return pltpu.VMEM(shape, dtype)

    return dict(
        gain=vm(1, C, dtype=F32), tgt=vm(1, TR, dtype=jnp.int32),
        k=vm(KJ, HD), v=vm(KJ, HD), wo=vm(HD, C), res=vm(R, C), w=vm(VP, C),
        q_all=vm(NS, TR, HD), s=vm(R, KJ, dtype=F32),
        acc_send=vm(NS, TR, HD), acc_recv=vm(NS, TR, HD),
        st_send=vm(NS, 8, 128, dtype=F32), st_recv=vm(NS, 8, 128, dtype=F32),
        full_send=vm(NS, TR, HD, dtype=F32), full_recv=vm(NS, TR, HD, dtype=F32), att_full=vm(TR, HD, dtype=F32),
        att_all=vm(NS, TR, HD), stat_all=vm(NS, 8, 128, dtype=F32),
        mix_send=vm(NV, RB, C), mix_recv=vm(NV, RB, C), mixed=vm(RB, C, dtype=F32),
        mg=vm(NV, RB, C), sq=vm(NS, 8, 128, dtype=F32), inv=vm(NV, 8, 128, dtype=F32),
        cw_send=vm(H, 2, TR, VH, dtype=F32), cw_recv=vm(H, 2, TR, VH, dtype=F32),
        cc_send=vm(H, 2, TR, VH, dtype=F32), cc_recv=vm(H, 2, TR, VH, dtype=F32),
        logits=vm(TR, VP, dtype=F32), stats=vm(NV, 8, 128, dtype=F32),
        normed=vm(R, C), g_all=vm(NS, 4, TR, VP // 4),
        loss=vm(NS, 8, 128, dtype=F32), loss1=vm(2, 8, 128, dtype=F32),
        loss2=vm(2, 8, 128, dtype=F32),
        hid_send=vm(NV, RB, C), hid_recv=vm(NV, RB, C), along=vm(NV, 8, 128, dtype=F32),
        mgrad=vm(NV, RB, C), ag_send=vm(NS, TR, HD), ag_recv=vm(NS, TR, HD),
        ag_all=vm(NS, TR, HD), delta=vm(NS, 8, 128, dtype=F32),
        hg_send=vm(2, VP // 4, C), hg_recv=vm(2, VP // 4, C), hg_own=vm(2, VP // 4, C),
        hg_pair=vm(2, VP // 4, C), hg_far=vm(2, VP // 4, C), fin=vm(4, VP // 4, C),
        kg=vm(KJ, HD, dtype=F32), vg=vm(KJ, HD, dtype=F32),
        ssem=pltpu.SemaphoreType.DMA((80,)), rsem=pltpu.SemaphoreType.DMA((80,)),
        lsem=pltpu.SemaphoreType.DMA((14,)),
    )


def body(sizes, queries, enc_keys, enc_values, enc_lengths, out_proj, residual, norm_gain, head_weight, targets):
    ND, NS, NV = sizes
    TR = queries.shape[1]
    KJ = enc_keys.shape[1]
    C, V = head_weight.shape
    VP = (V + 511) // 512 * 512
    cfg = (NS, NV, TR, KJ, C, V, VP, ND * TR * NS)
    vmem = pl.BlockSpec(memory_space=pltpu.VMEM)
    hbm = pl.BlockSpec(memory_space=pltpu.HBM)
    call = pl.pallas_call(
        functools.partial(kernel, cfg),
        out_shape=(
            jax.ShapeDtypeStruct((1, 1), F32),
            jax.ShapeDtypeStruct((V, C), BF16),
            jax.ShapeDtypeStruct((KJ, HDIM), F32),
            jax.ShapeDtypeStruct((KJ, HDIM), F32),
        ),
        in_specs=[hbm, hbm, hbm, pl.BlockSpec(memory_space=pltpu.SMEM), hbm, hbm, hbm, hbm, hbm],
        out_specs=(vmem, hbm, hbm, hbm),
        scratch_shapes=list(scratch_list(cfg).values()),
        compiler_params=pltpu.CompilerParams(
            collective_id=0, has_side_effects=True, vmem_limit_bytes=63 * 1024 * 1024),
    )
    loss, hg, kg, vg = call(
        queries[0], enc_keys[0], enc_values[0], enc_lengths, out_proj, residual[0],
        norm_gain.reshape(1, C), head_weight.T, targets)
    return (loss.reshape(()), hg.T, kg[None], vg[None])


def solution(mesh):
    placed = (
        P("dp", "seq", "vocab"),
        P("dp", "seq", "vocab"),
        P("dp", "seq", "vocab"),
        P("dp"),
        P("vocab", "seq"),
        P("dp", None, "seq"),
        P("seq"),
        P("seq", "vocab"),
        P("dp", "seq"),
    )
    sizes = (mesh.shape["dp"], mesh.shape["seq"], mesh.shape["vocab"])
    return jax.shard_map(
        functools.partial(body, sizes),
        mesh=mesh,
        in_specs=placed,
        out_specs=(P(), P("seq", "vocab"), P("dp", "seq", "vocab"), P("dp", "seq", "vocab")),
        check_vma=False,
    )
```

```python
import functools
import types

import jax
import jax.numpy as jnp
from jax import lax
from jax.experimental import pallas as pl
from jax.experimental.pallas import tpu as pltpu
from jax.sharding import PartitionSpec as P

HDIM = 256
ZW = 0.0001
EPS = 1e-06
MESH = pl.DeviceIdType.MESH
F32 = jnp.float32
BF16 = jnp.bfloat16


def dot(a, b, ca, cb):
    return lax.dot_general(a, b, (((ca,), (cb,)), ((), ())), preferred_element_type=F32)


def eye(n, m):
    return lax.broadcasted_iota(jnp.int32, (n, m), 0) == lax.broadcasted_iota(jnp.int32, (n, m), 1)


def to_row(col, n):
    return jnp.sum(jnp.where(eye(n, 128), jnp.broadcast_to(col, (n, 128)), 0.0), axis=0, keepdims=True)


def to_col(row, n):
    return jnp.sum(jnp.where(eye(n, 128), jnp.broadcast_to(row, (n, 128)), 0.0), axis=1, keepdims=True)


def sub_pick(rows):
    sub = lax.broadcasted_iota(jnp.int32, (8, 128), 0)
    tile = jnp.zeros((8, 128), F32)
    for i, row in enumerate(rows):
        tile = jnp.where(sub == i, row, tile)
    return tile


def kernel(cfg, q_hbm, k_hbm, v_hbm, ln, wo_hbm, res_hbm, gain_hbm, w_hbm, tgt_hbm, out_loss, out_hg, out_kg, out_vg, *scratch):
    NS, NV, TR, KJ, C, V, VP, batch_rows = cfg
    b = types.SimpleNamespace(**dict(zip(scratch_list(cfg), scratch)))
    HD = HDIM
    R = TR * NS
    RB = R // NV
    NB = TR // RB
    H = NS // 2
    VH = VP // 2
    D = C * NS
    scale = HD ** (-0.5)
    md, ms, mv = lax.axis_index("dp"), lax.axis_index("seq"), lax.axis_index("vocab")
    core = lax.rem(md, 2)
    zlo = md // 2
    mate = md + 1 - 2 * core
    zmate = lax.rem(md + 2, 4)
    right, left = lax.rem(ms + 1, NS), lax.rem(ms + NS - 1, NS)
    ssem, rsem = b.ssem, b.rsem
    used = [0]

    def sem():
        used[0] += 1
        return ssem.at[used[0] - 1], rsem.at[used[0] - 1]

    def push(src, dst, axis, to, sems):
        copy = pltpu.make_async_remote_copy(
            src_ref=src, dst_ref=dst, send_sem=sems[0], recv_sem=sems[1],
            device_id={axis: to}, device_id_type=MESH)
        copy.start()
        return copy

    drains = []

    def wait_bytes(ref, one):
        pltpu.make_async_copy(ref, ref, one).wait()

    NX = min(4, NV)
    NZ = NV // NX
    vx, vz = lax.rem(mv, NX), mv // NX
    seq_steps = sorted(range(1, NS), key=lambda a: -min(a, NS - a))
    vocab_steps = sorted(
        [(a, c) for a in range(NZ) for c in range(NX) if a or c],
        key=lambda d: -(2 * min(d[0], NZ - d[0]) + min(d[1], NX - d[1])))

    def others(axis):
        if axis == "seq":
            return [lax.rem(ms + a, NS) for a in seq_steps]
        return [lax.rem(vz + a, NZ) * NX + lax.rem(vx + c, NX) for a, c in vocab_steps]

    def spread(src, dst, axis):
        me, n = (ms, NS) if axis == "seq" else (mv, NV)
        sems = sem()
        for to in others(axis):
            push(src, dst.at[me], axis, to, sems)
        rest = dst.at[pl.ds(0, n - 1)]
        drains.append((rest, sems[0]))
        return lambda: wait_bytes(rest, sems[1])

    def scatter(src, dst, axis):
        n = NS if axis == "seq" else NV
        sems = sem()
        for i, to in enumerate(others(axis)):
            push(src.at[to], dst.at[i], axis, to, sems)
        rest = dst.at[pl.ds(0, n - 1)]
        drains.append((rest, sems[0]))
        return lambda: wait_bytes(rest, sems[1])

    def one(src, dst, axis, to):
        copy = push(src, dst, axis, to, sem())
        drains.append(copy)
        return copy.wait_recv

    barrier = pltpu.get_barrier_semaphore()
    for step in range(1, NS):
        pl.semaphore_signal(barrier, inc=1, device_id={"seq": lax.rem(ms + step, NS)}, device_id_type=MESH)
    for step in range(1, NV):
        pl.semaphore_signal(barrier, inc=1, device_id={"vocab": lax.rem(mv + step, NV)}, device_id_type=MESH)
    for to in (mate, zmate):
        pl.semaphore_signal(barrier, inc=1, device_id={"dp": to}, device_id_type=MESH)
    w = b.w
    k, v, wo, res, gain, tgt = b.k, b.v, b.wo, b.res, b.gain, b.tgt
    loads = []
    for i, (src, dst) in enumerate(
        ((q_hbm, b.q_all.at[ms]), (k_hbm, k), (v_hbm, v), (wo_hbm, wo), (res_hbm, res), (gain_hbm, gain),
         (tgt_hbm, tgt), (w_hbm, w.at[pl.ds(0, V)]))
    ):
        loads.append(pltpu.make_async_copy(src, dst, b.lsem.at[i]))
        loads[-1].start()
    pl.semaphore_wait(barrier, NS - 1 + NV - 1 + 2)

    got_q = spread(q_hbm, b.q_all, "seq")
    for load in loads[:3]:
        load.wait()
    got_q()
    q_rows = b.q_all[...].reshape(R, HD)
    s = dot(q_rows, k[...], 1, 1) * scale
    place = lax.broadcasted_iota(jnp.int32, (R, KJ), 1) + ms * KJ
    s = jnp.where(place < ln[0], s, -jnp.inf)
    b.s[...] = s
    peak = jnp.maximum(jnp.max(s, axis=1, keepdims=True), -1e30)
    e = jnp.exp(s - peak)
    total = jnp.sum(e, axis=1, keepdims=True)
    denom = jnp.maximum(total, 1e-30)
    e_top = e.astype(BF16)
    e_rest = e - e_top.astype(F32)
    e_mid = e_rest.astype(BF16)
    e_low = (e_rest - e_mid.astype(F32)).astype(BF16)
    acc = dot(e_top, v[...], 1, 0)
    b.acc_send[...] = (acc / denom).astype(BF16).reshape(NS, TR, HD)
    for i in range(NS):
        rows = slice(i * TR, (i + 1) * TR)
        b.st_send[i] = sub_pick([to_row(peak[rows], TR), to_row(total[rows], TR)])
    got_st = scatter(b.st_send, b.st_recv, "seq")
    got_acc = scatter(b.acc_send, b.acc_recv, "seq")
    acc = acc + (dot(e_mid, v[...], 1, 0) + dot(e_low, v[...], 1, 0))
    b.full_send[...] = (acc / denom).reshape(NS, TR, HD)
    for load in loads[3:]:
        load.wait()
    if V < VP:
        w[V:VP] = jnp.zeros((VP - V, C), BF16)
    got_st()
    b.st_recv[NS - 1] = b.st_send[ms]
    tiles = b.st_recv[...]
    top = jnp.max(tiles[:, 0:1], axis=0)
    parts = tiles[:, 1:2] * jnp.exp(tiles[:, 0:1] - top[None])
    whole = jnp.sum(parts, axis=0)
    shares = [to_col(parts[i] / whole, TR) for i in range(NS)]
    b.stat_all[ms] = sub_pick([top, whole])
    got_acc()
    att = b.acc_send[ms].astype(F32) * shares[NS - 1]
    for i in range(NS - 1):
        att = att + b.acc_recv[i].astype(F32) * shares[i]
    b.att_all[ms] = att.astype(BF16)
    got_att = spread(b.att_all.at[ms], b.att_all, "seq")
    got_stat = spread(b.stat_all.at[ms], b.stat_all, "seq")
    got_full = scatter(b.full_send, b.full_recv, "seq")
    got_att()

    mixed_part = dot(b.att_all[...].reshape(R, HD), wo[...], 1, 0)
    b.mix_send[...] = mixed_part.astype(BF16).reshape(NV, RB, C)
    got_mix = scatter(b.mix_send, b.mix_recv, "vocab")
    mine = res[pl.ds(pl.multiple_of(mv * RB, RB), RB), :].astype(F32)
    got_mix()
    mixed = mine + b.mix_send[mv].astype(F32)
    for i in range(NV - 1):
        mixed = mixed + b.mix_recv[i].astype(F32)
    b.mixed[...] = mixed
    b.mg[mv] = (mixed * gain[...]).astype(BF16)
    got_mg = spread(b.mg.at[mv], b.mg, "vocab")
    b.sq[ms] = sub_pick([to_row(jnp.sum(mixed * mixed, axis=1, keepdims=True), RB)])
    got_sq = spread(b.sq.at[ms], b.sq, "seq")
    got_sq()
    square = jnp.sum(b.sq[...], axis=0)[0:1]
    b.inv[mv] = sub_pick([lax.rsqrt(square / D + EPS)])
    got_inv = spread(b.inv.at[mv], b.inv, "vocab")
    got_mg()

    def rows_of(owner):
        return b.mg[pl.ds(owner * NB, NB)].reshape(TR, C)

    def at(distance):
        return lax.rem(ms + distance + NS, NS)

    half = [slice(0, VH), slice(VH, VP)]
    cw_send, cw_recv, cc_send, cc_recv = b.cw_send, b.cw_recv, b.cc_send, b.cc_recv
    cw_got, cc_got = {}, {}
    far = rows_of(at(H))
    for hh in range(2):
        block = dot(far, w[half[hh]], 1, 1)
        if hh == 0:
            cw_send[0, 0] = block
            cw_got[0, 0] = one(cw_send.at[0, 0], cw_recv.at[0, 0], "seq", right)
        else:
            cc_send[0, 1] = block
            cc_got[0, 1] = one(cc_send.at[0, 1], cc_recv.at[0, 1], "seq", left)
    for step in range(1, H):
        both = jnp.concatenate([rows_of(at(H - step)), rows_of(at(step - H))], axis=0)
        for hh in range(2):
            block = dot(both, w[half[hh]], 1, 1)
            cw_send[step, hh] = block[:TR]
            cc_send[step, hh] = block[TR:]
        for hh in range(2):
            for way in ((0, 1) if hh == 0 else (1, 0)):
                sends, recvs, got, to = ((cw_send, cw_recv, cw_got, right), (cc_send, cc_recv, cc_got, left))[way]
                if (step - 1, hh) in got:
                    got[step - 1, hh]()
                    sends[step, hh] = sends[step, hh] + recvs[step - 1, hh]
                got[step, hh] = one(sends.at[step, hh], recvs.at[step, hh], "seq", to)
    own = rows_of(ms)
    for hh in range(2):
        b.logits[:, half[hh]] = dot(own, w[half[hh]], 1, 1)
    got_full()
    att_full = b.full_send[ms] * shares[NS - 1]
    for i in range(NS - 1):
        att_full = att_full + b.full_recv[i] * shares[i]
    b.att_full[...] = att_full
    got_inv()
    normed = []
    for i in range(NV):
        normed.append(b.mg[i].astype(F32) * to_col(b.inv[i][0:1], RB))
    b.normed[zlo] = jnp.concatenate(normed, axis=0).astype(BF16)
    got_normed = one(b.normed.at[zlo], b.normed.at[zlo], "dp", zmate)
    inv_own = jnp.concatenate([to_col(b.inv[ms * NB + i][0:1], RB) for i in range(NB)], axis=0)
    for hh in range(2):
        block = b.logits[:, half[hh]]
        for got, recvs in ((cw_got, cw_recv), (cc_got, cc_recv)):
            if (H - 1, hh) in got:
                got[H - 1, hh]()
                block = block + recvs[H - 1, hh]
        block = block * inv_own
        if hh == 1:
            col = lax.broadcasted_iota(jnp.int32, (TR, VH), 1) + VH
            block = jnp.where(col < V, block, -jnp.inf)
        b.logits[:, half[hh]] = block

    logits = b.logits[...]
    tgt_col = to_col(jnp.concatenate([tgt[...].astype(F32), jnp.zeros((1, 128 - TR), F32)], axis=1), TR)
    tgt_col = tgt_col.astype(jnp.int32) - mv * V
    col = lax.broadcasted_iota(jnp.int32, (TR, VP), 1)
    hit = jnp.logical_and(col == tgt_col, col < V)
    row_peak = jnp.max(logits, axis=1, keepdims=True)
    row_sum = jnp.sum(jnp.exp(logits - row_peak), axis=1, keepdims=True)
    row_tgt = jnp.sum(jnp.where(hit, logits, 0.0), axis=1, keepdims=True)
    b.stats[mv] = sub_pick([to_row(x, TR) for x in (row_peak, row_sum, row_tgt)])
    got_stats = spread(b.stats.at[mv], b.stats, "vocab")
    got_stats()
    st = b.stats[...]
    tops = jnp.max(st[:, 0:1, :], axis=0)
    sums = jnp.sum(st[:, 1:2, :] * jnp.exp(st[:, 0:1, :] - tops[None]), axis=0)
    hits = jnp.sum(st[:, 2:3, :], axis=0)
    log_total = tops + jnp.log(sums)
    loss = log_total - hits + ZW * log_total * log_total
    lane = lax.broadcasted_iota(jnp.int32, (1, 128), 1)
    loss = jnp.where(lane < TR, loss, 0.0)
    lt = to_col(jnp.where(lane < TR, log_total, 0.0), TR)
    grad = jnp.exp(logits - lt) * (1.0 + 2.0 * ZW * lt) - hit.astype(F32)
    grad = grad.astype(BF16)
    g_all = b.g_all.at[zlo]
    g_far = b.g_all.at[1 - zlo]
    VQ = VP // 4
    along = jnp.sum(jnp.where(col < V, grad.astype(F32) * logits, 0.0), axis=1, keepdims=True)
    b.along[mv] = sub_pick([to_row(along, TR)])
    for i in range(4):
        g_all[ms, i] = grad[:, i * VQ:(i + 1) * VQ]

    got_z = one(g_all.at[ms], g_all.at[ms], "dp", zmate)

    def ring(buf):
        cw_got, cc_got = {}, {}

        def forward(step):
            for hh in range(2):
                for way in range(2):
                    got, to, owner = ((cw_got, right, at(-step)), (cc_got, left, at(step)))[way]
                    if step > 0:
                        got[step - 1, hh]()
                    if step == H - 1 and hh != way:
                        continue
                    piece = buf.at[owner, pl.ds(2 * hh, 2)]
                    got[step, hh] = one(piece, piece, "seq", to)

        def last():
            cw_got[H - 1, 0]()
            cc_got[H - 1, 1]()

        return forward, last

    forward, last = ring(g_all)
    far_forward, far_last = ring(g_far)
    hid_sems = sem()
    b_hid = b.hid_recv

    def hidden(owners):
        out = None
        for i in range(4):
            rows = jnp.concatenate([g_all[o, i] for o in owners], axis=0)
            term = dot(rows, w[i * VQ:(i + 1) * VQ], 1, 0)
            out = term if out is None else out + term
        out = out.astype(BF16)
        for i, o in enumerate(owners):
            b.hid_send[pl.ds(o * NB, NB)] = out[i * TR:(i + 1) * TR].reshape(NB, RB, C)
            for part in range(NB):
                to = o * NB + part

                @pl.when(to != mv)
                def _():
                    push(b.hid_send.at[to], b_hid.at[mv], "vocab", to, hid_sems)

    for step in range(H):
        forward(step)
        if step == 0:
            got_along = spread(b.along.at[mv], b.along, "vocab")
            hidden([ms])
        else:
            hidden([at(-step), at(step)])
        if step == min(1, H - 1):
            got_along()
            b.loss[ms] = sub_pick([loss, jnp.sum(b.along[...], axis=0)[0:1]])
            got_loss = spread(b.loss.at[ms], b.loss, "seq")
    got_z()
    far_forward(0)
    last()
    hidden([at(H)])
    for step in range(1, min(2, H)):
        far_forward(step)

    rest = b_hid.at[pl.ds(0, NV - 1)]
    drains.append((rest, hid_sems[0]))
    wait_bytes(rest, hid_sems[1])
    b_hid[mv] = b.hid_send[mv]
    gated = jnp.sum(b_hid[...].astype(F32), axis=0) * gain[...]
    got_loss()
    b.loss1[0] = jnp.sum(b.loss[...], axis=0)
    got_l1 = one(b.loss1.at[0], b.loss1.at[1], "dp", mate)
    row = lax.broadcasted_iota(jnp.int32, (RB, 128), 0) + lax.rem(mv, NB) * RB
    lane = lax.broadcasted_iota(jnp.int32, (RB, 128), 1)
    tile = jnp.broadcast_to(b.loss[mv // NB][1:2], (RB, 128))
    along = jnp.sum(jnp.where(row == lane, tile, 0.0), axis=1, keepdims=True)
    inv = to_col(b.inv[mv][0:1], RB)
    mixed_grad = gated * inv - b.mixed[...] * (inv * inv * along / D)
    b.mgrad[mv] = mixed_grad.astype(BF16)
    got_mgrad = spread(b.mgrad.at[mv], b.mgrad, "vocab")
    for step in range(2, H):
        far_forward(step)
    got_l1()
    b.loss2[0] = b.loss1[0] + b.loss1[1]
    got_l2 = one(b.loss2.at[0], b.loss2.at[1], "dp", zmate)
    got_stat()
    tops = jnp.concatenate([to_col(b.stat_all[i][0:1], TR) for i in range(NS)], axis=0)
    sums = jnp.concatenate([to_col(b.stat_all[i][1:2], TR) for i in range(NS)], axis=0)
    weights = jnp.exp(b.s[...] - tops) / sums
    b.s[...] = weights

    got_mgrad()
    ag_part = dot(b.mgrad[...].reshape(R, C), wo[...], 1, 1)
    b.ag_send[...] = ag_part.astype(BF16).reshape(NS, TR, HD)
    got_ag = scatter(b.ag_send, b.ag_recv, "seq")

    def head(quarter):
        return dot(b.g_all[:, :, quarter].reshape(2 * R, VQ), b.normed[...].reshape(2 * R, C), 0, 0).astype(BF16)

    far_last()
    got_normed()
    got_half = []
    for i in range(2):
        b.hg_send[i] = head(2 * (1 - core) + i)
        got_half.append(one(b.hg_send.at[i], b.hg_recv.at[i], "dp", mate))
    got_ag()
    ag = b.ag_send[ms].astype(F32)
    for i in range(NS - 1):
        ag = ag + b.ag_recv[i].astype(F32)
    ag = ag.astype(BF16)
    b.ag_all[ms] = ag
    got_ag_all = spread(b.ag_all.at[ms], b.ag_all, "seq")
    delta = jnp.sum(ag.astype(F32) * b.att_full[...], axis=1, keepdims=True)
    b.delta[ms] = sub_pick([to_row(delta, TR)])
    got_delta = spread(b.delta.at[ms], b.delta, "seq")
    fin = b.fin
    got_fin = []
    for i in range(2):
        b.hg_own[i] = head(2 * core + i)
        got_half[i]()
        piece = fin.at[2 * core + i]
        piece[...] = (b.hg_own[i].astype(F32) + b.hg_recv[i].astype(F32)).astype(BF16)
        got_fin.append(one(piece, piece, "dp", mate))
    got_ag_all()
    got_delta()
    ag_rows = b.ag_all[...].reshape(R, HD)
    prob_grad = dot(ag_rows, v[...], 1, 1)
    delta = jnp.concatenate([to_col(b.delta[i][0:1], TR) for i in range(NS)], axis=0)
    weights = b.s[...]
    score_grad = (weights * (prob_grad - delta) * scale).astype(BF16)
    b.kg[...] = dot(score_grad, b.q_all[...].reshape(R, HD), 0, 0)
    b.vg[...] = dot(weights.astype(BF16), ag_rows, 0, 0)
    stores = []
    for i, (src, dst) in enumerate(((b.kg, out_kg), (b.vg, out_vg))):
        stores.append(pltpu.make_async_copy(src, dst, b.lsem.at[12 + i]))
        stores[-1].start()
    got_l2()
    loss = (b.loss2[0] + b.loss2[1])[0:1]
    out_loss[...] = jnp.sum(loss, axis=1, keepdims=True) / batch_rows
    for got in got_fin:
        got()
    for i in range(4):
        size = min(VQ, V - i * VQ)
        if size > 0:
            store = pltpu.make_async_copy(fin.at[i, pl.ds(0, size)], out_hg.at[pl.ds(i * VQ, size)], b.lsem.at[8 + i])
            store.start()
            stores.append(store)
    for item in drains:
        if isinstance(item, tuple):
            wait_bytes(*item)
        else:
            item.wait_send()
    for store in stores:
        store.wait()


def scratch_list(cfg):
    NS, NV, TR, KJ, C, V, VP, batch_rows = cfg
    HD = HDIM
    R = TR * NS
    RB = R // NV
    H = NS // 2
    VH = VP // 2

    def vm(*shape, dtype=BF16):
        return pltpu.VMEM(shape, dtype)

    return dict(
        gain=vm(1, C, dtype=F32), tgt=vm(1, TR, dtype=jnp.int32),
        k=vm(KJ, HD), v=vm(KJ, HD), wo=vm(HD, C), res=vm(R, C), w=vm(VP, C),
        q_all=vm(NS, TR, HD), s=vm(R, KJ, dtype=F32),
        acc_send=vm(NS, TR, HD), acc_recv=vm(NS, TR, HD),
        st_send=vm(NS, 8, 128, dtype=F32), st_recv=vm(NS, 8, 128, dtype=F32),
        full_send=vm(NS, TR, HD, dtype=F32), full_recv=vm(NS, TR, HD, dtype=F32), att_full=vm(TR, HD, dtype=F32),
        att_all=vm(NS, TR, HD), stat_all=vm(NS, 8, 128, dtype=F32),
        mix_send=vm(NV, RB, C), mix_recv=vm(NV, RB, C), mixed=vm(RB, C, dtype=F32),
        mg=vm(NV, RB, C), sq=vm(NS, 8, 128, dtype=F32), inv=vm(NV, 8, 128, dtype=F32),
        cw_send=vm(H, 2, TR, VH, dtype=F32), cw_recv=vm(H, 2, TR, VH, dtype=F32),
        cc_send=vm(H, 2, TR, VH, dtype=F32), cc_recv=vm(H, 2, TR, VH, dtype=F32),
        logits=vm(TR, VP, dtype=F32), stats=vm(NV, 8, 128, dtype=F32),
        normed=vm(2, R, C), g_all=vm(2, NS, 4, TR, VP // 4),
        loss=vm(NS, 8, 128, dtype=F32), loss1=vm(2, 8, 128, dtype=F32),
        loss2=vm(2, 8, 128, dtype=F32),
        hid_send=vm(NV, RB, C), hid_recv=vm(NV, RB, C), along=vm(NV, 8, 128, dtype=F32),
        mgrad=vm(NV, RB, C), ag_send=vm(NS, TR, HD), ag_recv=vm(NS, TR, HD),
        ag_all=vm(NS, TR, HD), delta=vm(NS, 8, 128, dtype=F32),
        hg_send=vm(2, VP // 4, C), hg_recv=vm(2, VP // 4, C), hg_own=vm(2, VP // 4, C),
        fin=vm(4, VP // 4, C),
        kg=vm(KJ, HD, dtype=F32), vg=vm(KJ, HD, dtype=F32),
        ssem=pltpu.SemaphoreType.DMA((80,)), rsem=pltpu.SemaphoreType.DMA((80,)),
        lsem=pltpu.SemaphoreType.DMA((14,)),
    )


def body(sizes, queries, enc_keys, enc_values, enc_lengths, out_proj, residual, norm_gain, head_weight, targets):
    ND, NS, NV = sizes
    TR = queries.shape[1]
    KJ = enc_keys.shape[1]
    C, V = head_weight.shape
    VP = (V + 511) // 512 * 512
    cfg = (NS, NV, TR, KJ, C, V, VP, ND * TR * NS)
    vmem = pl.BlockSpec(memory_space=pltpu.VMEM)
    hbm = pl.BlockSpec(memory_space=pltpu.HBM)
    call = pl.pallas_call(
        functools.partial(kernel, cfg),
        out_shape=(
            jax.ShapeDtypeStruct((1, 1), F32),
            jax.ShapeDtypeStruct((V, C), BF16),
            jax.ShapeDtypeStruct((KJ, HDIM), F32),
            jax.ShapeDtypeStruct((KJ, HDIM), F32),
        ),
        in_specs=[hbm, hbm, hbm, pl.BlockSpec(memory_space=pltpu.SMEM), hbm, hbm, hbm, hbm, hbm],
        out_specs=(vmem, hbm, hbm, hbm),
        scratch_shapes=list(scratch_list(cfg).values()),
        compiler_params=pltpu.CompilerParams(
            collective_id=0, has_side_effects=True, vmem_limit_bytes=63 * 1024 * 1024),
    )
    loss, hg, kg, vg = call(
        queries[0], enc_keys[0], enc_values[0], enc_lengths, out_proj, residual[0],
        norm_gain.reshape(1, C), head_weight.T, targets)
    return (loss.reshape(()), hg.T, kg[None], vg[None])


def solution(mesh):
    placed = (
        P("dp", "seq", "vocab"),
        P("dp", "seq", "vocab"),
        P("dp", "seq", "vocab"),
        P("dp"),
        P("vocab", "seq"),
        P("dp", None, "seq"),
        P("seq"),
        P("seq", "vocab"),
        P("dp", "seq"),
    )
    sizes = (mesh.shape["dp"], mesh.shape["seq"], mesh.shape["vocab"])
    return jax.shard_map(
        functools.partial(body, sizes),
        mesh=mesh,
        in_specs=placed,
        out_specs=(P(), P("seq", "vocab"), P("dp", "seq", "vocab"), P("dp", "seq", "vocab")),
        check_vma=False,
    )
```

```python
import functools
import types

import jax
import jax.numpy as jnp
from jax import lax
from jax.experimental import pallas as pl
from jax.experimental.pallas import tpu as pltpu
from jax.sharding import PartitionSpec as P

HDIM = 256
ZW = 0.0001
EPS = 1e-06
MESH = pl.DeviceIdType.MESH
F32 = jnp.float32
SEMS = 128
BF16 = jnp.bfloat16


def dot(a, b, ca, cb):
    return lax.dot_general(a, b, (((ca,), (cb,)), ((), ())), preferred_element_type=F32)


def eye(n, m):
    return lax.broadcasted_iota(jnp.int32, (n, m), 0) == lax.broadcasted_iota(jnp.int32, (n, m), 1)


def to_row(col, n):
    return jnp.sum(jnp.where(eye(n, 128), jnp.broadcast_to(col, (n, 128)), 0.0), axis=0, keepdims=True)


def to_col(row, n):
    return jnp.sum(jnp.where(eye(n, 128), jnp.broadcast_to(row, (n, 128)), 0.0), axis=1, keepdims=True)


def sub_pick(rows):
    sub = lax.broadcasted_iota(jnp.int32, (8, 128), 0)
    tile = jnp.zeros((8, 128), F32)
    for i, row in enumerate(rows):
        tile = jnp.where(sub == i, row, tile)
    return tile


def kernel(cfg, q_hbm, k_hbm, v_hbm, ln, wo_hbm, res_hbm, gain_hbm, w_hbm, tgt_hbm, out_loss, out_hg, out_kg, out_vg, *scratch):
    NS, NV, TR, KJ, C, V, VP, batch_rows = cfg
    b = types.SimpleNamespace(**dict(zip(scratch_list(cfg), scratch)))
    HD = HDIM
    R = TR * NS
    RB = R // NV
    NB = TR // RB
    H = NS // 2
    D = C * NS
    scale = HD ** (-0.5)
    md, ms, mv = lax.axis_index("dp"), lax.axis_index("seq"), lax.axis_index("vocab")
    core = lax.rem(md, 2)
    zlo = md // 2
    mate = md + 1 - 2 * core
    zmate = lax.rem(md + 2, 4)
    right, left = lax.rem(ms + 1, NS), lax.rem(ms + NS - 1, NS)
    ssem, rsem = b.ssem, b.rsem
    used = [0]

    def sem():
        used[0] += 1
        return ssem.at[used[0] - 1], rsem.at[used[0] - 1]

    def push(src, dst, axis, to, sems):
        copy = pltpu.make_async_remote_copy(
            src_ref=src, dst_ref=dst, send_sem=sems[0], recv_sem=sems[1],
            device_id={axis: to}, device_id_type=MESH)
        copy.start()
        return copy

    drains = []

    def wait_bytes(ref, one):
        pltpu.make_async_copy(ref, ref, one).wait()

    NX = min(4, NV)
    NZ = NV // NX
    vx, vz = lax.rem(mv, NX), mv // NX
    seq_steps = sorted(range(1, NS), key=lambda a: -min(a, NS - a))
    vocab_steps = sorted(
        [(a, c) for a in range(NZ) for c in range(NX) if a or c],
        key=lambda d: -(2 * min(d[0], NZ - d[0]) + min(d[1], NX - d[1])))

    def others(axis):
        if axis == "seq":
            return [lax.rem(ms + a, NS) for a in seq_steps]
        return [lax.rem(vz + a, NZ) * NX + lax.rem(vx + c, NX) for a, c in vocab_steps]

    def spread(src, dst, axis):
        me, n = (ms, NS) if axis == "seq" else (mv, NV)
        sems = sem()
        for to in others(axis):
            push(src, dst.at[me], axis, to, sems)
        rest = dst.at[pl.ds(0, n - 1)]
        drains.append((rest, sems[0]))
        return lambda: wait_bytes(rest, sems[1])

    def scatter(src, dst, axis):
        n = NS if axis == "seq" else NV
        sems = sem()
        for i, to in enumerate(others(axis)):
            push(src.at[to], dst.at[i], axis, to, sems)
        rest = dst.at[pl.ds(0, n - 1)]
        drains.append((rest, sems[0]))
        return lambda: wait_bytes(rest, sems[1])

    def one(src, dst, axis, to):
        copy = push(src, dst, axis, to, sem())
        drains.append(copy)
        return copy.wait_recv

    barrier = pltpu.get_barrier_semaphore()
    for step in range(1, NS):
        pl.semaphore_signal(barrier, inc=1, device_id={"seq": lax.rem(ms + step, NS)}, device_id_type=MESH)
    for step in range(1, NV):
        pl.semaphore_signal(barrier, inc=1, device_id={"vocab": lax.rem(mv + step, NV)}, device_id_type=MESH)
    for to in (mate, zmate):
        pl.semaphore_signal(barrier, inc=1, device_id={"dp": to}, device_id_type=MESH)
    w = b.w
    k, v, wo, res, gain, tgt = b.k, b.v, b.wo, b.res, b.gain, b.tgt
    loads = []
    for i, (src, dst) in enumerate(
        ((q_hbm, b.q_all.at[ms]), (k_hbm, k), (v_hbm, v), (wo_hbm, wo), (res_hbm, res), (gain_hbm, gain),
         (tgt_hbm, tgt), (w_hbm, w.at[pl.ds(0, V)]))
    ):
        loads.append(pltpu.make_async_copy(src, dst, b.lsem.at[i]))
        loads[-1].start()
    pl.semaphore_wait(barrier, NS - 1 + NV - 1 + 2)

    got_q = spread(q_hbm, b.q_all, "seq")
    for load in loads[:3]:
        load.wait()
    got_q()
    q_rows = b.q_all[...].reshape(R, HD)
    s = dot(q_rows, k[...], 1, 1) * scale
    place = lax.broadcasted_iota(jnp.int32, (R, KJ), 1) + ms * KJ
    s = jnp.where(place < ln[0], s, -jnp.inf)
    b.s[...] = s
    peak = jnp.maximum(jnp.max(s, axis=1, keepdims=True), -1e30)
    e = jnp.exp(s - peak)
    total = jnp.sum(e, axis=1, keepdims=True)
    denom = jnp.maximum(total, 1e-30)
    e_top = e.astype(BF16)
    e_rest = e - e_top.astype(F32)
    e_mid = e_rest.astype(BF16)
    e_low = (e_rest - e_mid.astype(F32)).astype(BF16)
    acc = dot(e_top, v[...], 1, 0)
    b.acc_send[...] = (acc / denom).astype(BF16).reshape(NS, TR, HD)
    for i in range(NS):
        rows = slice(i * TR, (i + 1) * TR)
        b.st_send[i] = sub_pick([to_row(peak[rows], TR), to_row(total[rows], TR)])
    got_st = scatter(b.st_send, b.st_recv, "seq")
    got_acc = scatter(b.acc_send, b.acc_recv, "seq")
    acc = acc + (dot(e_mid, v[...], 1, 0) + dot(e_low, v[...], 1, 0))
    b.full_send[...] = (acc / denom).reshape(NS, TR, HD)
    for load in loads[3:]:
        load.wait()
    if V < VP:
        w[V:VP] = jnp.zeros((VP - V, C), BF16)
    got_st()
    b.st_recv[NS - 1] = b.st_send[ms]
    tiles = b.st_recv[...]
    top = jnp.max(tiles[:, 0:1], axis=0)
    parts = tiles[:, 1:2] * jnp.exp(tiles[:, 0:1] - top[None])
    whole = jnp.sum(parts, axis=0)
    shares = [to_col(parts[i] / whole, TR) for i in range(NS)]
    b.stat_all[ms] = sub_pick([top, whole])
    got_acc()
    att = b.acc_send[ms].astype(F32) * shares[NS - 1]
    for i in range(NS - 1):
        att = att + b.acc_recv[i].astype(F32) * shares[i]
    b.att_all[ms] = att.astype(BF16)
    got_att = spread(b.att_all.at[ms], b.att_all, "seq")
    got_stat = spread(b.stat_all.at[ms], b.stat_all, "seq")
    got_full = scatter(b.full_send, b.full_recv, "seq")
    got_att()

    mixed_part = dot(b.att_all[...].reshape(R, HD), wo[...], 1, 0)
    b.mix_send[...] = mixed_part.astype(BF16).reshape(NV, RB, C)
    got_mix = scatter(b.mix_send, b.mix_recv, "vocab")
    mine = res[pl.ds(pl.multiple_of(mv * RB, RB), RB), :].astype(F32)
    got_mix()
    mixed = mine + b.mix_send[mv].astype(F32)
    for i in range(NV - 1):
        mixed = mixed + b.mix_recv[i].astype(F32)
    b.mixed[...] = mixed
    b.mg[mv] = (mixed * gain[...]).astype(BF16)
    got_mg = spread(b.mg.at[mv], b.mg, "vocab")
    b.sq[ms] = sub_pick([to_row(jnp.sum(mixed * mixed, axis=1, keepdims=True), RB)])
    got_sq = spread(b.sq.at[ms], b.sq, "seq")
    got_sq()
    square = jnp.sum(b.sq[...], axis=0)[0:1]
    b.inv[mv] = sub_pick([lax.rsqrt(square / D + EPS)])
    got_inv = spread(b.inv.at[mv], b.inv, "vocab")
    got_mg()

    def rows_of(owner):
        return b.mg[pl.ds(owner * NB, NB)].reshape(TR, C)

    def at(distance):
        return lax.rem(ms + distance + NS, NS)

    VQ = VP // 4
    part = [slice(i * VQ, (i + 1) * VQ) for i in range(4)]
    order = ((0, 1, 2, 3), (2, 3, 0, 1))
    sends, recvs, gots = (b.cw_send, b.cc_send), (b.cw_recv, b.cc_recv), ({}, {})
    toward = (right, left)
    far = rows_of(at(H))
    for i in (0, 2, 1, 3):
        way = i // 2
        sends[way][0, i] = dot(far, w[part[i]], 1, 1)
        gots[way][0, i] = one(sends[way].at[0, i], recvs[way].at[0, i], "seq", toward[way])
    for step in range(1, H):
        both = jnp.concatenate([rows_of(at(H - step)), rows_of(at(step - H))], axis=0)
        for i in range(4):
            block = dot(both, w[part[i]], 1, 1)
            sends[0][step, i] = block[:TR]
            sends[1][step, i] = block[TR:]
        for n in range(4):
            for way in range(2):
                i = order[way][n]
                if (step - 1, i) in gots[way]:
                    gots[way][step - 1, i]()
                    sends[way][step, i] = sends[way][step, i] + recvs[way][step - 1, i]
                gots[way][step, i] = one(sends[way].at[step, i], recvs[way].at[step, i], "seq", toward[way])
    own = rows_of(ms)
    for i in range(4):
        b.logits[:, part[i]] = dot(own, w[part[i]], 1, 1)
    got_full()
    att_full = b.full_send[ms] * shares[NS - 1]
    for i in range(NS - 1):
        att_full = att_full + b.full_recv[i] * shares[i]
    b.att_full[...] = att_full
    got_inv()
    normed = []
    for i in range(NV):
        normed.append(b.mg[i].astype(F32) * to_col(b.inv[i][0:1], RB))
    b.normed[zlo] = jnp.concatenate(normed, axis=0).astype(BF16)
    got_normed = one(b.normed.at[zlo], b.normed.at[zlo], "dp", zmate)
    inv_own = jnp.concatenate([to_col(b.inv[ms * NB + i][0:1], RB) for i in range(NB)], axis=0)
    for i in range(4):
        block = b.logits[:, part[i]]
        for way in range(2):
            if (H - 1, i) in gots[way]:
                gots[way][H - 1, i]()
                block = block + recvs[way][H - 1, i]
        block = block * inv_own
        if (i + 1) * VQ > V:
            col = lax.broadcasted_iota(jnp.int32, (TR, VQ), 1) + i * VQ
            block = jnp.where(col < V, block, -jnp.inf)
        b.logits[:, part[i]] = block

    logits = b.logits[...]
    tgt_col = to_col(jnp.concatenate([tgt[...].astype(F32), jnp.zeros((1, 128 - TR), F32)], axis=1), TR)
    tgt_col = tgt_col.astype(jnp.int32) - mv * V
    col = lax.broadcasted_iota(jnp.int32, (TR, VP), 1)
    hit = jnp.logical_and(col == tgt_col, col < V)
    row_peak = jnp.max(logits, axis=1, keepdims=True)
    row_sum = jnp.sum(jnp.exp(logits - row_peak), axis=1, keepdims=True)
    row_tgt = jnp.sum(jnp.where(hit, logits, 0.0), axis=1, keepdims=True)
    b.stats[mv] = sub_pick([to_row(x, TR) for x in (row_peak, row_sum, row_tgt)])
    got_stats = spread(b.stats.at[mv], b.stats, "vocab")
    got_stats()
    st = b.stats[...]
    tops = jnp.max(st[:, 0:1, :], axis=0)
    sums = jnp.sum(st[:, 1:2, :] * jnp.exp(st[:, 0:1, :] - tops[None]), axis=0)
    hits = jnp.sum(st[:, 2:3, :], axis=0)
    log_total = tops + jnp.log(sums)
    loss = log_total - hits + ZW * log_total * log_total
    lane = lax.broadcasted_iota(jnp.int32, (1, 128), 1)
    loss = jnp.where(lane < TR, loss, 0.0)
    lt = to_col(jnp.where(lane < TR, log_total, 0.0), TR)
    grad = jnp.exp(logits - lt) * (1.0 + 2.0 * ZW * lt) - hit.astype(F32)
    grad = grad.astype(BF16)
    g_all = b.g_all.at[zlo]
    g_far = b.g_all.at[1 - zlo]
    along = jnp.sum(jnp.where(col < V, grad.astype(F32) * logits, 0.0), axis=1, keepdims=True)
    b.along[mv] = sub_pick([to_row(along, TR)])
    for i in range(4):
        g_all[ms, i] = grad[:, i * VQ:(i + 1) * VQ]

    got_z = one(g_all.at[ms], g_all.at[ms], "dp", zmate)

    def ring(buf):
        cw_got, cc_got = {}, {}

        def forward(step):
            for n in range(4):
                for way in range(2):
                    i = order[way][n]
                    got, owner = ((cw_got, at(-step)), (cc_got, at(step)))[way]
                    if step > 0:
                        got[step - 1, i]()
                    if step == H - 1 and i // 2 != way:
                        continue
                    piece = buf.at[owner, i]
                    got[step, i] = one(piece, piece, "seq", toward[way])

        def last():
            for i in range(4):
                (cw_got, cc_got)[i // 2][H - 1, i]()

        return forward, last

    forward, last = ring(g_all)
    far_forward, far_last = ring(g_far)
    hid_sems = sem()
    b_hid = b.hid_recv

    def hidden(owners):
        out = None
        for i in range(4):
            rows = jnp.concatenate([g_all[o, i] for o in owners], axis=0)
            term = dot(rows, w[i * VQ:(i + 1) * VQ], 1, 0)
            out = term if out is None else out + term
        out = out.astype(BF16)
        for i, o in enumerate(owners):
            b.hid_send[pl.ds(o * NB, NB)] = out[i * TR:(i + 1) * TR].reshape(NB, RB, C)
            for part in range(NB):
                to = o * NB + part

                @pl.when(to != mv)
                def _():
                    push(b.hid_send.at[to], b_hid.at[mv], "vocab", to, hid_sems)

    for step in range(H):
        forward(step)
        if step == 0:
            got_along = spread(b.along.at[mv], b.along, "vocab")
            hidden([ms])
        else:
            hidden([at(-step), at(step)])
        if step == min(1, H - 1):
            got_along()
            b.loss[ms] = sub_pick([loss, jnp.sum(b.along[...], axis=0)[0:1]])
            got_loss = spread(b.loss.at[ms], b.loss, "seq")
    got_z()
    far_forward(0)
    last()
    hidden([at(H)])
    for step in range(1, min(2, H)):
        far_forward(step)

    rest = b_hid.at[pl.ds(0, NV - 1)]
    drains.append((rest, hid_sems[0]))
    wait_bytes(rest, hid_sems[1])
    b_hid[mv] = b.hid_send[mv]
    gated = jnp.sum(b_hid[...].astype(F32), axis=0) * gain[...]
    got_loss()
    b.loss1[0] = jnp.sum(b.loss[...], axis=0)
    got_l1 = one(b.loss1.at[0], b.loss1.at[1], "dp", mate)
    row = lax.broadcasted_iota(jnp.int32, (RB, 128), 0) + lax.rem(mv, NB) * RB
    lane = lax.broadcasted_iota(jnp.int32, (RB, 128), 1)
    tile = jnp.broadcast_to(b.loss[mv // NB][1:2], (RB, 128))
    along = jnp.sum(jnp.where(row == lane, tile, 0.0), axis=1, keepdims=True)
    inv = to_col(b.inv[mv][0:1], RB)
    mixed_grad = gated * inv - b.mixed[...] * (inv * inv * along / D)
    b.mgrad[mv] = mixed_grad.astype(BF16)
    got_mgrad = spread(b.mgrad.at[mv], b.mgrad, "vocab")
    for step in range(2, H):
        far_forward(step)
    got_l1()
    b.loss2[0] = b.loss1[0] + b.loss1[1]
    got_l2 = one(b.loss2.at[0], b.loss2.at[1], "dp", zmate)
    got_stat()
    tops = jnp.concatenate([to_col(b.stat_all[i][0:1], TR) for i in range(NS)], axis=0)
    sums = jnp.concatenate([to_col(b.stat_all[i][1:2], TR) for i in range(NS)], axis=0)
    weights = jnp.exp(b.s[...] - tops) / sums
    b.s[...] = weights

    got_mgrad()
    ag_part = dot(b.mgrad[...].reshape(R, C), wo[...], 1, 1)
    b.ag_send[...] = ag_part.astype(BF16).reshape(NS, TR, HD)
    got_ag = scatter(b.ag_send, b.ag_recv, "seq")

    def head(quarter):
        return dot(b.g_all[:, :, quarter].reshape(2 * R, VQ), b.normed[...].reshape(2 * R, C), 0, 0).astype(BF16)

    far_last()
    got_normed()
    got_half = []
    for i in range(2):
        b.hg_send[i] = head(2 * (1 - core) + i)
        got_half.append(one(b.hg_send.at[i], b.hg_recv.at[i], "dp", mate))
    got_ag()
    ag = b.ag_send[ms].astype(F32)
    for i in range(NS - 1):
        ag = ag + b.ag_recv[i].astype(F32)
    ag = ag.astype(BF16)
    b.ag_all[ms] = ag
    got_ag_all = spread(b.ag_all.at[ms], b.ag_all, "seq")
    delta = jnp.sum(ag.astype(F32) * b.att_full[...], axis=1, keepdims=True)
    b.delta[ms] = sub_pick([to_row(delta, TR)])
    got_delta = spread(b.delta.at[ms], b.delta, "seq")
    fin = b.fin
    got_fin = []
    for i in range(2):
        b.hg_own[i] = head(2 * core + i)
        got_half[i]()
        piece = fin.at[2 * core + i]
        piece[...] = (b.hg_own[i].astype(F32) + b.hg_recv[i].astype(F32)).astype(BF16)
        got_fin.append(one(piece, piece, "dp", mate))
    got_ag_all()
    got_delta()
    ag_rows = b.ag_all[...].reshape(R, HD)
    prob_grad = dot(ag_rows, v[...], 1, 1)
    delta = jnp.concatenate([to_col(b.delta[i][0:1], TR) for i in range(NS)], axis=0)
    weights = b.s[...]
    score_grad = (weights * (prob_grad - delta) * scale).astype(BF16)
    b.kg[...] = dot(score_grad, b.q_all[...].reshape(R, HD), 0, 0)
    b.vg[...] = dot(weights.astype(BF16), ag_rows, 0, 0)
    stores = []
    for i, (src, dst) in enumerate(((b.kg, out_kg), (b.vg, out_vg))):
        stores.append(pltpu.make_async_copy(src, dst, b.lsem.at[12 + i]))
        stores[-1].start()
    got_l2()
    loss = (b.loss2[0] + b.loss2[1])[0:1]
    out_loss[...] = jnp.sum(loss, axis=1, keepdims=True) / batch_rows
    for got in got_fin:
        got()
    for i in range(4):
        size = min(VQ, V - i * VQ)
        if size > 0:
            store = pltpu.make_async_copy(fin.at[i, pl.ds(0, size)], out_hg.at[pl.ds(i * VQ, size)], b.lsem.at[8 + i])
            store.start()
            stores.append(store)
    for item in drains:
        if isinstance(item, tuple):
            wait_bytes(*item)
        else:
            item.wait_send()
    for store in stores:
        store.wait()


def scratch_list(cfg):
    NS, NV, TR, KJ, C, V, VP, batch_rows = cfg
    HD = HDIM
    R = TR * NS
    RB = R // NV
    H = NS // 2

    def vm(*shape, dtype=BF16):
        return pltpu.VMEM(shape, dtype)

    return dict(
        gain=vm(1, C, dtype=F32), tgt=vm(1, TR, dtype=jnp.int32),
        k=vm(KJ, HD), v=vm(KJ, HD), wo=vm(HD, C), res=vm(R, C), w=vm(VP, C),
        q_all=vm(NS, TR, HD), s=vm(R, KJ, dtype=F32),
        acc_send=vm(NS, TR, HD), acc_recv=vm(NS, TR, HD),
        st_send=vm(NS, 8, 128, dtype=F32), st_recv=vm(NS, 8, 128, dtype=F32),
        full_send=vm(NS, TR, HD, dtype=F32), full_recv=vm(NS, TR, HD, dtype=F32), att_full=vm(TR, HD, dtype=F32),
        att_all=vm(NS, TR, HD), stat_all=vm(NS, 8, 128, dtype=F32),
        mix_send=vm(NV, RB, C), mix_recv=vm(NV, RB, C), mixed=vm(RB, C, dtype=F32),
        mg=vm(NV, RB, C), sq=vm(NS, 8, 128, dtype=F32), inv=vm(NV, 8, 128, dtype=F32),
        cw_send=vm(H, 4, TR, VP // 4, dtype=F32), cw_recv=vm(H, 4, TR, VP // 4, dtype=F32),
        cc_send=vm(H, 4, TR, VP // 4, dtype=F32), cc_recv=vm(H, 4, TR, VP // 4, dtype=F32),
        logits=vm(TR, VP, dtype=F32), stats=vm(NV, 8, 128, dtype=F32),
        normed=vm(2, R, C), g_all=vm(2, NS, 4, TR, VP // 4),
        loss=vm(NS, 8, 128, dtype=F32), loss1=vm(2, 8, 128, dtype=F32),
        loss2=vm(2, 8, 128, dtype=F32),
        hid_send=vm(NV, RB, C), hid_recv=vm(NV, RB, C), along=vm(NV, 8, 128, dtype=F32),
        mgrad=vm(NV, RB, C), ag_send=vm(NS, TR, HD), ag_recv=vm(NS, TR, HD),
        ag_all=vm(NS, TR, HD), delta=vm(NS, 8, 128, dtype=F32),
        hg_send=vm(2, VP // 4, C), hg_recv=vm(2, VP // 4, C), hg_own=vm(2, VP // 4, C),
        fin=vm(4, VP // 4, C),
        kg=vm(KJ, HD, dtype=F32), vg=vm(KJ, HD, dtype=F32),
        ssem=pltpu.SemaphoreType.DMA((SEMS,)), rsem=pltpu.SemaphoreType.DMA((SEMS,)),
        lsem=pltpu.SemaphoreType.DMA((14,)),
    )


def tail(hg, kg, vg, hg_out, kg_out, vg_out, hg_mid, kg_mid, vg_mid, sems, sems_out):
    rows = hg.shape[0] // 64 * 16
    steps = [(hg, hg_mid, hg_out, pl.ds(i * rows, rows if i < 3 else hg.shape[0] - 3 * rows)) for i in range(4)]
    steps += [(kg, kg_mid, kg_out, pl.ds(0, kg.shape[0])), (vg, vg_mid, vg_out, pl.ds(0, vg.shape[0]))]
    loads = [pltpu.make_async_copy(a.at[d], m.at[d], sems.at[i]) for i, (a, m, _, d) in enumerate(steps)]
    stores = [pltpu.make_async_copy(m.at[d], o.at[d], sems_out.at[i]) for i, (_, m, o, d) in enumerate(steps)]
    for load in loads:
        load.start()
    for load, store in zip(loads, stores):
        load.wait()
        store.start()
    for store in stores:
        store.wait()


def body(sizes, queries, enc_keys, enc_values, enc_lengths, out_proj, residual, norm_gain, head_weight, targets):
    ND, NS, NV = sizes
    TR = queries.shape[1]
    KJ = enc_keys.shape[1]
    C, V = head_weight.shape
    VP = (V + 511) // 512 * 512
    cfg = (NS, NV, TR, KJ, C, V, VP, ND * TR * NS)
    vmem = pl.BlockSpec(memory_space=pltpu.VMEM)
    hbm = pl.BlockSpec(memory_space=pltpu.HBM)
    call = pl.pallas_call(
        functools.partial(kernel, cfg),
        out_shape=(
            jax.ShapeDtypeStruct((1, 1), F32),
            jax.ShapeDtypeStruct((V, C), BF16),
            jax.ShapeDtypeStruct((KJ, HDIM), F32),
            jax.ShapeDtypeStruct((KJ, HDIM), F32),
        ),
        in_specs=[hbm, hbm, hbm, pl.BlockSpec(memory_space=pltpu.SMEM), hbm, hbm, hbm, hbm, hbm],
        out_specs=(vmem, hbm, hbm, hbm),
        scratch_shapes=list(scratch_list(cfg).values()),
        compiler_params=pltpu.CompilerParams(
            collective_id=0, has_side_effects=True, vmem_limit_bytes=63 * 1024 * 1024),
    )
    loss, hg, kg, vg = call(
        queries[0], enc_keys[0], enc_values[0], enc_lengths, out_proj, residual[0],
        norm_gain.reshape(1, C), head_weight.T, targets)
    hg, kg, vg = pl.pallas_call(
        tail,
        out_shape=tuple(jax.ShapeDtypeStruct(x.shape, x.dtype) for x in (hg, kg, vg)),
        in_specs=[hbm] * 3,
        out_specs=(hbm,) * 3,
        scratch_shapes=[pltpu.VMEM(x.shape, x.dtype) for x in (hg, kg, vg)] + [pltpu.SemaphoreType.DMA((6,))] * 2,
        compiler_params=pltpu.CompilerParams(vmem_limit_bytes=63 * 1024 * 1024),
    )(hg, kg, vg)
    return (loss.reshape(()), hg.T, kg[None], vg[None])


def solution(mesh):
    placed = (
        P("dp", "seq", "vocab"),
        P("dp", "seq", "vocab"),
        P("dp", "seq", "vocab"),
        P("dp"),
        P("vocab", "seq"),
        P("dp", None, "seq"),
        P("seq"),
        P("seq", "vocab"),
        P("dp", "seq"),
    )
    sizes = (mesh.shape["dp"], mesh.shape["seq"], mesh.shape["vocab"])
    return jax.shard_map(
        functools.partial(body, sizes),
        mesh=mesh,
        in_specs=placed,
        out_specs=(P(), P("seq", "vocab"), P("dp", "seq", "vocab"), P("dp", "seq", "vocab")),
        check_vma=False,
    )
```

```python
import functools
import types

import jax
import jax.numpy as jnp
from jax import lax
from jax.experimental import pallas as pl
from jax.experimental.pallas import tpu as pltpu
from jax.sharding import PartitionSpec as P

HDIM = 256
ZW = 0.0001
EPS = 1e-06
MESH = pl.DeviceIdType.MESH
F32 = jnp.float32
SEMS = 128
BF16 = jnp.bfloat16


def dot(a, b, ca, cb):
    return lax.dot_general(a, b, (((ca,), (cb,)), ((), ())), preferred_element_type=F32)


def eye(n, m):
    return lax.broadcasted_iota(jnp.int32, (n, m), 0) == lax.broadcasted_iota(jnp.int32, (n, m), 1)


def to_row(col, n):
    return jnp.sum(jnp.where(eye(n, 128), jnp.broadcast_to(col, (n, 128)), 0.0), axis=0, keepdims=True)


def to_col(row, n):
    return jnp.sum(jnp.where(eye(n, 128), jnp.broadcast_to(row, (n, 128)), 0.0), axis=1, keepdims=True)


def sub_pick(rows):
    sub = lax.broadcasted_iota(jnp.int32, (8, 128), 0)
    tile = jnp.zeros((8, 128), F32)
    for i, row in enumerate(rows):
        tile = jnp.where(sub == i, row, tile)
    return tile


def kernel(cfg, q_hbm, k_hbm, v_hbm, ln, wo_hbm, res_hbm, gain_hbm, w_hbm, tgt_hbm, out_loss, out_hg, out_kg, out_vg, *scratch):
    NS, NV, TR, KJ, C, V, VP, batch_rows = cfg
    b = types.SimpleNamespace(**dict(zip(scratch_list(cfg), scratch)))
    HD = HDIM
    R = TR * NS
    RB = R // NV
    NB = TR // RB
    H = NS // 2
    D = C * NS
    scale = HD ** (-0.5)
    md, ms, mv = lax.axis_index("dp"), lax.axis_index("seq"), lax.axis_index("vocab")
    core = lax.rem(md, 2)
    zlo = md // 2
    mate = md + 1 - 2 * core
    zmate = lax.rem(md + 2, 4)
    right, left = lax.rem(ms + 1, NS), lax.rem(ms + NS - 1, NS)
    ssem, rsem = b.ssem, b.rsem
    used = [0]

    def sem():
        used[0] += 1
        return ssem.at[used[0] - 1], rsem.at[used[0] - 1]

    def push(src, dst, axis, to, sems):
        copy = pltpu.make_async_remote_copy(
            src_ref=src, dst_ref=dst, send_sem=sems[0], recv_sem=sems[1],
            device_id={axis: to}, device_id_type=MESH)
        copy.start()
        return copy

    drains = []

    def wait_bytes(ref, one):
        pltpu.make_async_copy(ref, ref, one).wait()

    NX = min(4, NV)
    NZ = NV // NX
    vx, vz = lax.rem(mv, NX), mv // NX
    seq_steps = sorted(range(1, NS), key=lambda a: -min(a, NS - a))
    vocab_steps = sorted(
        [(a, c) for a in range(NZ) for c in range(NX) if a or c],
        key=lambda d: -(2 * min(d[0], NZ - d[0]) + min(d[1], NX - d[1])))

    def others(axis):
        if axis == "seq":
            return [lax.rem(ms + a, NS) for a in seq_steps]
        return [lax.rem(vz + a, NZ) * NX + lax.rem(vx + c, NX) for a, c in vocab_steps]

    def spread(src, dst, axis):
        me, n = (ms, NS) if axis == "seq" else (mv, NV)
        sems = sem()
        for to in others(axis):
            push(src, dst.at[me], axis, to, sems)
        rest = dst.at[pl.ds(0, n - 1)]
        drains.append((rest, sems[0]))
        return lambda: wait_bytes(rest, sems[1])

    def scatter(src, dst, axis):
        n = NS if axis == "seq" else NV
        sems = sem()
        for i, to in enumerate(others(axis)):
            push(src.at[to], dst.at[i], axis, to, sems)
        rest = dst.at[pl.ds(0, n - 1)]
        drains.append((rest, sems[0]))
        return lambda: wait_bytes(rest, sems[1])

    def one(src, dst, axis, to):
        copy = push(src, dst, axis, to, sem())
        drains.append(copy)
        return copy.wait_recv

    barrier = pltpu.get_barrier_semaphore()
    for step in range(1, NS):
        pl.semaphore_signal(barrier, inc=1, device_id={"seq": lax.rem(ms + step, NS)}, device_id_type=MESH)
    for step in range(1, NV):
        pl.semaphore_signal(barrier, inc=1, device_id={"vocab": lax.rem(mv + step, NV)}, device_id_type=MESH)
    for to in (mate, zmate):
        pl.semaphore_signal(barrier, inc=1, device_id={"dp": to}, device_id_type=MESH)
    w = b.w
    k, v, wo, res, gain, tgt = b.k, b.v, b.wo, b.res, b.gain, b.tgt
    loads = []
    for i, (src, dst) in enumerate(
        ((q_hbm, b.q_all.at[ms]), (k_hbm, k), (v_hbm, v), (wo_hbm, wo), (res_hbm, res), (gain_hbm, gain),
         (tgt_hbm, tgt), (w_hbm, w.at[pl.ds(0, V)]))
    ):
        loads.append(pltpu.make_async_copy(src, dst, b.lsem.at[i]))
        loads[-1].start()
    pl.semaphore_wait(barrier, NS - 1 + NV - 1 + 2)

    got_q = spread(q_hbm, b.q_all, "seq")
    for load in loads[:3]:
        load.wait()
    got_q()
    q_rows = b.q_all[...].reshape(R, HD)
    s = dot(q_rows, k[...], 1, 1) * scale
    place = lax.broadcasted_iota(jnp.int32, (R, KJ), 1) + ms * KJ
    s = jnp.where(place < ln[0], s, -jnp.inf)
    b.s[...] = s
    peak = jnp.maximum(jnp.max(s, axis=1, keepdims=True), -1e30)
    e = jnp.exp(s - peak)
    total = jnp.sum(e, axis=1, keepdims=True)
    denom = jnp.maximum(total, 1e-30)
    e_top = e.astype(BF16)
    e_rest = e - e_top.astype(F32)
    e_mid = e_rest.astype(BF16)
    e_low = (e_rest - e_mid.astype(F32)).astype(BF16)
    acc = dot(e_top, v[...], 1, 0)
    b.acc_send[...] = (acc / denom).astype(BF16).reshape(NS, TR, HD)
    for i in range(NS):
        rows = slice(i * TR, (i + 1) * TR)
        b.st_send[i] = sub_pick([to_row(peak[rows], TR), to_row(total[rows], TR)])
    got_st = scatter(b.st_send, b.st_recv, "seq")
    got_acc = scatter(b.acc_send, b.acc_recv, "seq")
    acc = acc + (dot(e_mid, v[...], 1, 0) + dot(e_low, v[...], 1, 0))
    b.full_send[...] = (acc / denom).reshape(NS, TR, HD)
    for load in loads[3:]:
        load.wait()
    if V < VP:
        w[V:VP] = jnp.zeros((VP - V, C), BF16)
    got_st()
    b.st_recv[NS - 1] = b.st_send[ms]
    tiles = b.st_recv[...]
    top = jnp.max(tiles[:, 0:1], axis=0)
    parts = tiles[:, 1:2] * jnp.exp(tiles[:, 0:1] - top[None])
    whole = jnp.sum(parts, axis=0)
    shares = [to_col(parts[i] / whole, TR) for i in range(NS)]
    b.stat_all[ms] = sub_pick([top, whole])
    got_acc()
    att = b.acc_send[ms].astype(F32) * shares[NS - 1]
    for i in range(NS - 1):
        att = att + b.acc_recv[i].astype(F32) * shares[i]
    b.att_all[ms] = att.astype(BF16)
    got_att = spread(b.att_all.at[ms], b.att_all, "seq")
    got_att()

    mixed_part = dot(b.att_all[...].reshape(R, HD), wo[...], 1, 0)
    b.mix_send[...] = mixed_part.astype(BF16).reshape(NV, RB, C)
    got_mix = scatter(b.mix_send, b.mix_recv, "vocab")
    mine = res[pl.ds(pl.multiple_of(mv * RB, RB), RB), :].astype(F32)
    got_mix()
    mixed = mine + b.mix_send[mv].astype(F32)
    for i in range(NV - 1):
        mixed = mixed + b.mix_recv[i].astype(F32)
    b.mixed[...] = mixed
    b.mg[mv] = (mixed * gain[...]).astype(BF16)
    got_mg = spread(b.mg.at[mv], b.mg, "vocab")
    b.sq[ms] = sub_pick([to_row(jnp.sum(mixed * mixed, axis=1, keepdims=True), RB)])
    got_sq = spread(b.sq.at[ms], b.sq, "seq")
    got_stat = spread(b.stat_all.at[ms], b.stat_all, "seq")
    got_full = scatter(b.full_send, b.full_recv, "seq")
    got_mg()

    def rows_of(owner):
        return b.mg[pl.ds(owner * NB, NB)].reshape(TR, C)

    def at(distance):
        return lax.rem(ms + distance + NS, NS)

    VQ = VP // 4
    part = [slice(i * VQ, (i + 1) * VQ) for i in range(4)]
    order = ((0, 1, 2, 3), (2, 3, 0, 1))
    sends, recvs, gots = (b.cw_send, b.cc_send), (b.cw_recv, b.cc_recv), ({}, {})
    toward = (right, left)
    far = rows_of(at(H))
    for i in (0, 2, 1, 3):
        way = i // 2
        sends[way][0, i] = dot(far, w[part[i]], 1, 1)
        gots[way][0, i] = one(sends[way].at[0, i], recvs[way].at[0, i], "seq", toward[way])
    got_sq()
    square = jnp.sum(b.sq[...], axis=0)[0:1]
    b.inv[mv] = sub_pick([lax.rsqrt(square / D + EPS)])
    got_inv = spread(b.inv.at[mv], b.inv, "vocab")
    for step in range(1, H):
        both = jnp.concatenate([rows_of(at(H - step)), rows_of(at(step - H))], axis=0)
        for i in range(4):
            block = dot(both, w[part[i]], 1, 1)
            sends[0][step, i] = block[:TR]
            sends[1][step, i] = block[TR:]
        for n in range(4):
            for way in range(2):
                i = order[way][n]
                if (step - 1, i) in gots[way]:
                    gots[way][step - 1, i]()
                    sends[way][step, i] = sends[way][step, i] + recvs[way][step - 1, i]
                gots[way][step, i] = one(sends[way].at[step, i], recvs[way].at[step, i], "seq", toward[way])
    own = rows_of(ms)
    for i in range(4):
        b.logits[:, part[i]] = dot(own, w[part[i]], 1, 1)
    got_full()
    att_full = b.full_send[ms] * shares[NS - 1]
    for i in range(NS - 1):
        att_full = att_full + b.full_recv[i] * shares[i]
    b.att_full[...] = att_full
    got_inv()
    normed = []
    for i in range(NV):
        normed.append(b.mg[i].astype(F32) * to_col(b.inv[i][0:1], RB))
    b.normed[zlo] = jnp.concatenate(normed, axis=0).astype(BF16)
    inv_own = jnp.concatenate([to_col(b.inv[ms * NB + i][0:1], RB) for i in range(NB)], axis=0)
    for i in range(4):
        block = b.logits[:, part[i]]
        for way in range(2):
            if (H - 1, i) in gots[way]:
                gots[way][H - 1, i]()
                block = block + recvs[way][H - 1, i]
        block = block * inv_own
        if (i + 1) * VQ > V:
            col = lax.broadcasted_iota(jnp.int32, (TR, VQ), 1) + i * VQ
            block = jnp.where(col < V, block, -jnp.inf)
        b.logits[:, part[i]] = block

    logits = b.logits[...]
    tgt_col = to_col(jnp.concatenate([tgt[...].astype(F32), jnp.zeros((1, 128 - TR), F32)], axis=1), TR)
    tgt_col = tgt_col.astype(jnp.int32) - mv * V
    col = lax.broadcasted_iota(jnp.int32, (TR, VP), 1)
    hit = jnp.logical_and(col == tgt_col, col < V)
    row_peak = jnp.max(logits, axis=1, keepdims=True)
    row_sum = jnp.sum(jnp.exp(logits - row_peak), axis=1, keepdims=True)
    row_tgt = jnp.sum(jnp.where(hit, logits, 0.0), axis=1, keepdims=True)
    b.stats[mv] = sub_pick([to_row(x, TR) for x in (row_peak, row_sum, row_tgt)])
    got_stats = spread(b.stats.at[mv], b.stats, "vocab")
    got_stats()
    st = b.stats[...]
    tops = jnp.max(st[:, 0:1, :], axis=0)
    sums = jnp.sum(st[:, 1:2, :] * jnp.exp(st[:, 0:1, :] - tops[None]), axis=0)
    hits = jnp.sum(st[:, 2:3, :], axis=0)
    log_total = tops + jnp.log(sums)
    loss = log_total - hits + ZW * log_total * log_total
    lane = lax.broadcasted_iota(jnp.int32, (1, 128), 1)
    loss = jnp.where(lane < TR, loss, 0.0)
    lt = to_col(jnp.where(lane < TR, log_total, 0.0), TR)
    grad = jnp.exp(logits - lt) * (1.0 + 2.0 * ZW * lt) - hit.astype(F32)
    grad = grad.astype(BF16)
    g_all = b.g_all.at[zlo]
    g_far = b.g_all.at[1 - zlo]
    along = jnp.sum(jnp.where(col < V, grad.astype(F32) * logits, 0.0), axis=1, keepdims=True)
    b.along[mv] = sub_pick([to_row(along, TR)])
    for i in range(4):
        g_all[ms, i] = grad[:, i * VQ:(i + 1) * VQ]


    def ring(buf):
        cw_got, cc_got = {}, {}

        def forward(step):
            for n in range(4):
                for way in range(2):
                    i = order[way][n]
                    got, owner = ((cw_got, at(-step)), (cc_got, at(step)))[way]
                    if step > 0:
                        got[step - 1, i]()
                    if step == H - 1 and i // 2 != way:
                        continue
                    piece = buf.at[owner, i]
                    got[step, i] = one(piece, piece, "seq", toward[way])

        def last():
            for i in range(4):
                (cw_got, cc_got)[i // 2][H - 1, i]()

        return forward, last

    forward, last = ring(g_all)
    far_forward, far_last = ring(g_far)
    hid_sems = sem()
    b_hid = b.hid_recv

    def hidden(owners):
        out = None
        for i in range(4):
            rows = jnp.concatenate([g_all[o, i] for o in owners], axis=0)
            term = dot(rows, w[i * VQ:(i + 1) * VQ], 1, 0)
            out = term if out is None else out + term
        out = out.astype(BF16)
        for i, o in enumerate(owners):
            b.hid_send[pl.ds(o * NB, NB)] = out[i * TR:(i + 1) * TR].reshape(NB, RB, C)
            for part in range(NB):
                to = o * NB + part

                @pl.when(to != mv)
                def _():
                    push(b.hid_send.at[to], b_hid.at[mv], "vocab", to, hid_sems)

    for step in range(H):
        forward(step)
        if step == 0:
            got_along = spread(b.along.at[mv], b.along, "vocab")
            got_z = one(g_all.at[ms], g_all.at[ms], "dp", zmate)
            got_normed = one(b.normed.at[zlo], b.normed.at[zlo], "dp", zmate)
            hidden([ms])
        else:
            hidden([at(-step), at(step)])
        if step == min(2, H - 1):
            got_along()
            b.loss[ms] = sub_pick([loss, jnp.sum(b.along[...], axis=0)[0:1]])
            got_loss = spread(b.loss.at[ms], b.loss, "seq")
    last()
    hidden([at(H)])
    got_z()
    far_forward(0)
    for step in range(1, min(2, H)):
        far_forward(step)

    rest = b_hid.at[pl.ds(0, NV - 1)]
    drains.append((rest, hid_sems[0]))
    wait_bytes(rest, hid_sems[1])
    b_hid[mv] = b.hid_send[mv]
    gated = jnp.sum(b_hid[...].astype(F32), axis=0) * gain[...]
    got_loss()
    b.loss1[0] = jnp.sum(b.loss[...], axis=0)
    got_l1 = one(b.loss1.at[0], b.loss1.at[1], "dp", mate)
    row = lax.broadcasted_iota(jnp.int32, (RB, 128), 0) + lax.rem(mv, NB) * RB
    lane = lax.broadcasted_iota(jnp.int32, (RB, 128), 1)
    tile = jnp.broadcast_to(b.loss[mv // NB][1:2], (RB, 128))
    along = jnp.sum(jnp.where(row == lane, tile, 0.0), axis=1, keepdims=True)
    inv = to_col(b.inv[mv][0:1], RB)
    mixed_grad = gated * inv - b.mixed[...] * (inv * inv * along / D)
    b.mgrad[mv] = mixed_grad.astype(BF16)
    got_mgrad = spread(b.mgrad.at[mv], b.mgrad, "vocab")
    for step in range(2, H):
        far_forward(step)
    got_l1()
    b.loss2[0] = b.loss1[0] + b.loss1[1]
    got_l2 = one(b.loss2.at[0], b.loss2.at[1], "dp", zmate)
    got_stat()
    tops = jnp.concatenate([to_col(b.stat_all[i][0:1], TR) for i in range(NS)], axis=0)
    sums = jnp.concatenate([to_col(b.stat_all[i][1:2], TR) for i in range(NS)], axis=0)
    weights = jnp.exp(b.s[...] - tops) / sums
    b.s[...] = weights

    got_mgrad()
    ag_part = dot(b.mgrad[...].reshape(R, C), wo[...], 1, 1)
    b.ag_send[...] = ag_part.astype(BF16).reshape(NS, TR, HD)
    got_ag = scatter(b.ag_send, b.ag_recv, "seq")

    def head(quarter):
        return dot(b.g_all[:, :, quarter].reshape(2 * R, VQ), b.normed[...].reshape(2 * R, C), 0, 0).astype(BF16)

    far_last()
    got_normed()
    got_half = []
    for i in range(2):
        b.hg_send[i] = head(2 * (1 - core) + i)
        got_half.append(one(b.hg_send.at[i], b.hg_recv.at[i], "dp", mate))
    got_ag()
    ag = b.ag_send[ms].astype(F32)
    for i in range(NS - 1):
        ag = ag + b.ag_recv[i].astype(F32)
    ag = ag.astype(BF16)
    b.ag_all[ms] = ag
    got_ag_all = spread(b.ag_all.at[ms], b.ag_all, "seq")
    delta = jnp.sum(ag.astype(F32) * b.att_full[...], axis=1, keepdims=True)
    b.delta[ms] = sub_pick([to_row(delta, TR)])
    got_delta = spread(b.delta.at[ms], b.delta, "seq")
    fin = b.fin
    got_fin = []
    for i in range(2):
        b.hg_own[i] = head(2 * core + i)
        got_half[i]()
        piece = fin.at[2 * core + i]
        piece[...] = (b.hg_own[i].astype(F32) + b.hg_recv[i].astype(F32)).astype(BF16)
        got_fin.append(one(piece, piece, "dp", mate))
    got_ag_all()
    got_delta()
    ag_rows = b.ag_all[...].reshape(R, HD)
    prob_grad = dot(ag_rows, v[...], 1, 1)
    delta = jnp.concatenate([to_col(b.delta[i][0:1], TR) for i in range(NS)], axis=0)
    weights = b.s[...]
    score_grad = (weights * (prob_grad - delta) * scale).astype(BF16)
    b.kg[...] = dot(score_grad, b.q_all[...].reshape(R, HD), 0, 0)
    b.vg[...] = dot(weights.astype(BF16), ag_rows, 0, 0)
    stores = []
    for i, (src, dst) in enumerate(((b.kg, out_kg), (b.vg, out_vg))):
        stores.append(pltpu.make_async_copy(src, dst, b.lsem.at[12 + i]))
        stores[-1].start()
    got_l2()
    loss = (b.loss2[0] + b.loss2[1])[0:1]
    out_loss[...] = jnp.sum(loss, axis=1, keepdims=True) / batch_rows
    for got in got_fin:
        got()
    for i in range(4):
        size = min(VQ, V - i * VQ)
        if size > 0:
            store = pltpu.make_async_copy(fin.at[i, pl.ds(0, size)], out_hg.at[pl.ds(i * VQ, size)], b.lsem.at[8 + i])
            store.start()
            stores.append(store)
    for item in drains:
        if isinstance(item, tuple):
            wait_bytes(*item)
        else:
            item.wait_send()
    for store in stores:
        store.wait()


def scratch_list(cfg):
    NS, NV, TR, KJ, C, V, VP, batch_rows = cfg
    HD = HDIM
    R = TR * NS
    RB = R // NV
    H = NS // 2

    def vm(*shape, dtype=BF16):
        return pltpu.VMEM(shape, dtype)

    return dict(
        gain=vm(1, C, dtype=F32), tgt=vm(1, TR, dtype=jnp.int32),
        k=vm(KJ, HD), v=vm(KJ, HD), wo=vm(HD, C), res=vm(R, C), w=vm(VP, C),
        q_all=vm(NS, TR, HD), s=vm(R, KJ, dtype=F32),
        acc_send=vm(NS, TR, HD), acc_recv=vm(NS, TR, HD),
        st_send=vm(NS, 8, 128, dtype=F32), st_recv=vm(NS, 8, 128, dtype=F32),
        full_send=vm(NS, TR, HD, dtype=F32), full_recv=vm(NS, TR, HD, dtype=F32), att_full=vm(TR, HD, dtype=F32),
        att_all=vm(NS, TR, HD), stat_all=vm(NS, 8, 128, dtype=F32),
        mix_send=vm(NV, RB, C), mix_recv=vm(NV, RB, C), mixed=vm(RB, C, dtype=F32),
        mg=vm(NV, RB, C), sq=vm(NS, 8, 128, dtype=F32), inv=vm(NV, 8, 128, dtype=F32),
        cw_send=vm(H, 4, TR, VP // 4, dtype=F32), cw_recv=vm(H, 4, TR, VP // 4, dtype=F32),
        cc_send=vm(H, 4, TR, VP // 4, dtype=F32), cc_recv=vm(H, 4, TR, VP // 4, dtype=F32),
        logits=vm(TR, VP, dtype=F32), stats=vm(NV, 8, 128, dtype=F32),
        normed=vm(2, R, C), g_all=vm(2, NS, 4, TR, VP // 4),
        loss=vm(NS, 8, 128, dtype=F32), loss1=vm(2, 8, 128, dtype=F32),
        loss2=vm(2, 8, 128, dtype=F32),
        hid_send=vm(NV, RB, C), hid_recv=vm(NV, RB, C), along=vm(NV, 8, 128, dtype=F32),
        mgrad=vm(NV, RB, C), ag_send=vm(NS, TR, HD), ag_recv=vm(NS, TR, HD),
        ag_all=vm(NS, TR, HD), delta=vm(NS, 8, 128, dtype=F32),
        hg_send=vm(2, VP // 4, C), hg_recv=vm(2, VP // 4, C), hg_own=vm(2, VP // 4, C),
        fin=vm(4, VP // 4, C),
        kg=vm(KJ, HD, dtype=F32), vg=vm(KJ, HD, dtype=F32),
        ssem=pltpu.SemaphoreType.DMA((SEMS,)), rsem=pltpu.SemaphoreType.DMA((SEMS,)),
        lsem=pltpu.SemaphoreType.DMA((14,)),
    )


def tail(hg, kg, vg, hg_out, kg_out, vg_out, hg_mid, kg_mid, vg_mid, sems, sems_out):
    rows = hg.shape[0] // 64 * 16
    steps = [(hg, hg_mid, hg_out, pl.ds(i * rows, rows if i < 3 else hg.shape[0] - 3 * rows)) for i in range(4)]
    steps += [(kg, kg_mid, kg_out, pl.ds(0, kg.shape[0])), (vg, vg_mid, vg_out, pl.ds(0, vg.shape[0]))]
    loads = [pltpu.make_async_copy(a.at[d], m.at[d], sems.at[i]) for i, (a, m, _, d) in enumerate(steps)]
    stores = [pltpu.make_async_copy(m.at[d], o.at[d], sems_out.at[i]) for i, (_, m, o, d) in enumerate(steps)]
    for load in loads:
        load.start()
    for load, store in zip(loads, stores):
        load.wait()
        store.start()
    for store in stores:
        store.wait()


def body(sizes, queries, enc_keys, enc_values, enc_lengths, out_proj, residual, norm_gain, head_weight, targets):
    ND, NS, NV = sizes
    TR = queries.shape[1]
    KJ = enc_keys.shape[1]
    C, V = head_weight.shape
    VP = (V + 511) // 512 * 512
    cfg = (NS, NV, TR, KJ, C, V, VP, ND * TR * NS)
    vmem = pl.BlockSpec(memory_space=pltpu.VMEM)
    hbm = pl.BlockSpec(memory_space=pltpu.HBM)
    call = pl.pallas_call(
        functools.partial(kernel, cfg),
        out_shape=(
            jax.ShapeDtypeStruct((1, 1), F32),
            jax.ShapeDtypeStruct((V, C), BF16),
            jax.ShapeDtypeStruct((KJ, HDIM), F32),
            jax.ShapeDtypeStruct((KJ, HDIM), F32),
        ),
        in_specs=[hbm, hbm, hbm, pl.BlockSpec(memory_space=pltpu.SMEM), hbm, hbm, hbm, hbm, hbm],
        out_specs=(vmem, hbm, hbm, hbm),
        scratch_shapes=list(scratch_list(cfg).values()),
        compiler_params=pltpu.CompilerParams(
            collective_id=0, has_side_effects=True, vmem_limit_bytes=63 * 1024 * 1024),
    )
    loss, hg, kg, vg = call(
        queries[0], enc_keys[0], enc_values[0], enc_lengths, out_proj, residual[0],
        norm_gain.reshape(1, C), head_weight.T, targets)
    hg, kg, vg = pl.pallas_call(
        tail,
        out_shape=tuple(jax.ShapeDtypeStruct(x.shape, x.dtype) for x in (hg, kg, vg)),
        in_specs=[hbm] * 3,
        out_specs=(hbm,) * 3,
        scratch_shapes=[pltpu.VMEM(x.shape, x.dtype) for x in (hg, kg, vg)] + [pltpu.SemaphoreType.DMA((6,))] * 2,
        compiler_params=pltpu.CompilerParams(vmem_limit_bytes=63 * 1024 * 1024),
    )(hg, kg, vg)
    return (loss.reshape(()), hg.T, kg[None], vg[None])


def solution(mesh):
    placed = (
        P("dp", "seq", "vocab"),
        P("dp", "seq", "vocab"),
        P("dp", "seq", "vocab"),
        P("dp"),
        P("vocab", "seq"),
        P("dp", None, "seq"),
        P("seq"),
        P("seq", "vocab"),
        P("dp", "seq"),
    )
    sizes = (mesh.shape["dp"], mesh.shape["seq"], mesh.shape["vocab"])
    return jax.shard_map(
        functools.partial(body, sizes),
        mesh=mesh,
        in_specs=placed,
        out_specs=(P(), P("seq", "vocab"), P("dp", "seq", "vocab"), P("dp", "seq", "vocab")),
        check_vma=False,
    )
```
